32 devices in a mesh: seq: 8 (over z, y), ffn: 4 (over x, core).
Axes of the slice: x: 2, y: 2, z: 4, core: 2. Of those that a mesh axis runs over, the one named last changes fastest.
Arguments:
- child_feat: bfloat16 [4096, 1024], P('seq'), may hold values from -6 to 6
- parent_feat: bfloat16 [512, 1024], P('seq'), may hold values from -6 to 6
- child_parent: int32 [4096], P('seq'), may hold values from 0 to 63
- owner: int32 [4096, 1], P('seq'), may hold values from 0 to 7; in each aligned block of 512 rows (0 to 511, 512 to 1023, ...) at most 128 rows name the same one
- log_gate: float32 [16, 8192], P('ffn', 'seq'), may hold values from -1 to 0
- norm_gain: bfloat16 [1024], replicated, may hold values from 0.3984375 to 1.59375
- w_query: bfloat16 [1024, 1024], P(None, 'ffn'), may hold values from -0.1875 to 0.1875
- w_key: bfloat16 [1024, 1024], P(None, 'ffn'), may hold values from -0.1875 to 0.1875
- w_value: bfloat16 [1024, 1024], P(None, 'ffn'), may hold values from -0.1875 to 0.1875
- head_gain: bfloat16 [1024], P('ffn'), may hold values from 0.25 to 1.75
- w_out: bfloat16 [1024, 1024], P('ffn'), may hold values from -0.1875 to 0.1875
- ffn_gain: bfloat16 [1024], replicated, may hold values from 0.3984375 to 1.59375
- w_up: bfloat16 [1024, 4096], P(None, 'ffn'), may hold values from -0.1875 to 0.1875
- w_down: bfloat16 [4096, 1024], P('ffn'), may hold values from -0.09375 to 0.09375
Outputs:
- child_out: bfloat16 [4096, 1024], P('seq', 'ffn')
The draws below stay inside these ranges and needn't reach their ends.
Inputs may be any that keep to these rules, and one draw needn't show every extreme that they name: The parent of child i is row (i // 512) * 64 + child_parent[i] of parent_feat. Among the 512 children of one index of seq, at most 128 name the same owner, and in every draw some owner is named exactly 128 times by some block.
All inputs are finite; a program needn't handle non-finite values.
Results may differ from the reference program's by a relative error of at most 0.013.
Values may be sent and summed in bfloat16 or wider, within the bound.
No kernel may reach another device: no remote copies, remote signals or barrier semaphores. Data moves between devices by JAX's collectives and lax.ppermute only.
A program may use at most 64 MiB of HBM per device.

```python
import math
import jax
import jax.numpy as jnp
import numpy as np
from jax import lax

D = 1024
HEAD_TOTAL = 16
HD = 64
FF = 4096
TOK_DEV = 512
PAR_DEV = 64
CAP = 128
SLOT_DEV = 1024
TOKENS = 4096
PARENTS = 512
SLOT_TOTAL = 8192
N_SEQ = 8
N_FFN = 4


def draw_log_gate(key, part):
    random_subkeys = jax.random.split(key, 7)
    fast_share = 0.5
    forgetful = jax.random.uniform(random_subkeys[0], (HEAD_TOTAL,)) < fast_share
    fast_rate = 1.0 / jax.random.uniform(random_subkeys[1], (HEAD_TOTAL,), minval=30.0, maxval=50.0)
    slow_rate = math.log(10.0) * jax.random.uniform(random_subkeys[2], (HEAD_TOTAL,), minval=0.05, maxval=0.15) / SLOT_TOTAL
    retain_rate = jnp.where(forgetful, fast_rate, slow_rate)
    block_count = SLOT_TOTAL // SLOT_DEV
    per_block = jnp.exp(jax.random.uniform(random_subkeys[3], (HEAD_TOTAL, block_count), minval=-math.log(2.0), maxval=math.log(2.0)))
    spread_out = jnp.repeat(per_block, SLOT_DEV, axis=1)
    roughness = jnp.exp(jax.random.uniform(random_subkeys[4], (HEAD_TOTAL, SLOT_TOTAL), minval=-math.log(2.0), maxval=math.log(2.0)))
    gate_logarithms = -retain_rate[:, None] * spread_out * roughness
    surge_position = jax.random.randint(random_subkeys[5], (HEAD_TOTAL, 3), 0, SLOT_TOTAL)
    surge_penalty = jnp.log(jax.random.uniform(random_subkeys[6], (HEAD_TOTAL, 3), minval=0.55, maxval=0.75))
    slot_numbers = jnp.arange(SLOT_TOTAL, dtype=jnp.int32)
    surge_flags = slot_numbers[None, None, :] == surge_position[:, :, None]
    gate_logarithms = gate_logarithms + jnp.sum(jnp.where(surge_flags, surge_penalty[:, :, None], 0.0), axis=1)
    return jnp.maximum(gate_logarithms, -1.0).astype(jnp.float32)


def plant(values, rng, smallest, largest):
    longest = values.shape.index(max(values.shape))
    spots = []
    for shift in (0, 1):
        where = [jax.random.randint(jax.random.fold_in(rng, axis), (), 0, length) for axis, length in enumerate(values.shape)]
        where[longest] = (where[longest] + shift) % values.shape[longest]
        spots.append(tuple(where))
    return values.at[spots[0]].set(smallest).at[spots[1]].set(largest)


def steps_of(own_key, extent, cuts, low, high):
    factor_of, own = 1.0, jax.random.fold_in(own_key, 6)
    for axis_at, shards_of in cuts:
        steps = jnp.exp(jax.random.uniform(jax.random.fold_in(own, axis_at), (shards_of,), jnp.float32, low / len(cuts), high / len(cuts)))
        factor_of = factor_of * jnp.repeat(steps, extent[axis_at] // shards_of).reshape([-1 if axis == axis_at else 1 for axis in range(len(extent))])
    return factor_of


def routed_block(stream_key, own, number, rows, count, top, limit, slope):
    order = jax.random.permutation(stream_key, count)
    packed, usual = shares(count, rows * top, limit, slope, True), shares(count, rows * top, limit, slope, False)
    places = jnp.arange(count)

    def named(lengths, offset_by):
        used = int((lengths > 0).sum())
        fixed = max(1, used // 4)
        shifted = fixed + (places - fixed + offset_by * (used - fixed)) % max(1, count - fixed)
        return jnp.zeros((count,), jnp.int32).at[order[jnp.where(places < fixed, places, shifted)]].set(jnp.asarray(lengths, jnp.int32))

    lengths = jnp.where(number % 4 == 0, named(packed, number // 4), named(usual, number - number // 4 - 1))
    mixed = jax.random.permutation(jax.random.fold_in(own, 3), count)
    source_of, taker = mixed[0:count // 2 * 2:2], mixed[1:count // 2 * 2:2]
    slack = jnp.minimum(lengths[source_of] - 1, limit - lengths[taker]) // 2
    slack = jnp.where((source_of == order[0]) | (taker == order[0]) | (lengths[taker] == 0), 0, jnp.maximum(slack, 0))
    shifted = jax.random.randint(jax.random.fold_in(own, 4), (count // 2,), 0, 1 << 20) % (slack + 1)
    lengths = lengths.at[source_of].add(-shifted).at[taker].add(shifted)
    items = jnp.searchsorted(jnp.cumsum(lengths), jnp.arange(rows * top), side="right").astype(jnp.int32)
    grid = items.reshape(top, rows).T
    grid = grid[jax.random.permutation(jax.random.fold_in(own, 1), rows)]
    offset_by = jax.random.randint(jax.random.fold_in(own, 2), (rows, 1), 0, top)
    return jnp.take_along_axis(grid, (jnp.arange(top)[None, :] + offset_by) % top, axis=1)


def shares(amount, total, limit, lean, full):
    portions = [(1 << 20) // math.isqrt(rank ** lean) + 1 for rank in range(1, amount + 1)]
    largest = limit if full else min(limit, max(-(-total // amount), total * portions[0] // sum(portions)))
    least = 1 if total - largest >= amount - 1 else 0
    counts, surplus = [largest] + [least] * (amount - 1), total - largest - least * (amount - 1)
    while surplus > 0:
        free = [i for i in range(1, amount) if counts[i] < largest] or [i for i in range(1, amount) if counts[i] < limit]
        mass, left = sum([portions[i] for i in free]), surplus
        for i in free:
            more = min(limit - counts[i], max(1, left * portions[i] // mass), surplus)
            counts[i] = counts[i] + more
            surplus = surplus - more
    return np.array(counts)


def normal_values(own_key, shape, width, reach, shards=(), kind=jnp.bfloat16):
    array = width * jax.random.normal(own_key, shape, jnp.float32)
    if shards:
        array = array * steps_of(own_key, shape, shards, -0.22, 0.18)
    return jnp.clip(array, -reach, reach).astype(kind)


def setup_inputs(seed: int = 0) -> dict:
    arg_keys = jax.random.split(jax.random.key(seed), 15)
    child_feat = normal_values(arg_keys[0], (TOKENS, D), 1.0, 6.0, ((0, 8),))
    parent_feat = normal_values(arg_keys[1], (PARENTS, D), 0.7, 6.0, ((0, 8),))
    child_parent = plant(jax.random.randint(arg_keys[2], (TOKENS,), 0, PAR_DEV), jax.random.fold_in(arg_keys[2], 1), 0, PAR_DEV - 1).astype(jnp.int32)
    owner_keys = jax.random.split(jax.random.fold_in(arg_keys[3], 1), TOKENS // TOK_DEV)
    owner_turns = jax.random.permutation(jax.random.fold_in(arg_keys[3], 3), TOKENS // TOK_DEV)
    owner = jax.vmap(lambda own, number: routed_block(jax.random.fold_in(arg_keys[3], 2), own, number, TOK_DEV, N_SEQ, 1, CAP, 1))(owner_keys, owner_turns).reshape((TOKENS, 1))
    log_gate = draw_log_gate(jax.random.fold_in(arg_keys[14], 71), 0)
    norm_gain = jnp.clip(1.0 + 0.12 * jax.random.normal(arg_keys[5], (D,), jnp.float32), 0.3984375, 1.59375).astype(jnp.bfloat16)
    w_query = normal_values(arg_keys[6], (D, HEAD_TOTAL * HD), D ** -0.5, 0.1875, ((1, 4),))
    w_key = normal_values(arg_keys[7], (D, HEAD_TOTAL * HD), D ** -0.5, 0.1875, ((1, 4),))
    w_value = normal_values(arg_keys[8], (D, HEAD_TOTAL * HD), D ** -0.5, 0.1875, ((1, 4),))
    head_gain = jnp.clip(1.0 + 0.15 * jax.random.normal(arg_keys[9], (HEAD_TOTAL * HD,), jnp.float32), 0.25, 1.75).astype(jnp.bfloat16)
    w_out = normal_values(arg_keys[10], (HEAD_TOTAL * HD, D), (HEAD_TOTAL * HD) ** -0.5, 0.1875, ((0, 4),))
    ffn_gain = jnp.clip(1.0 + 0.12 * jax.random.normal(arg_keys[11], (D,), jnp.float32), 0.3984375, 1.59375).astype(jnp.bfloat16)
    w_up = normal_values(arg_keys[12], (D, FF), D ** -0.5, 0.1875, ((1, 4),))
    w_down = normal_values(arg_keys[13], (FF, D), FF ** -0.5, 0.09375, ((0, 4),))
    return dict(child_feat=child_feat, parent_feat=parent_feat, child_parent=child_parent, owner=owner, log_gate=log_gate, norm_gain=norm_gain, w_query=w_query, w_key=w_key, w_value=w_value, head_gain=head_gain, w_out=w_out, ffn_gain=ffn_gain, w_up=w_up, w_down=w_down)


EPSILON = 1e-05
PRECISE = lax.Precision.HIGHEST

def rounded(values):
    return lax.optimization_barrier(values.astype(jnp.bfloat16)).astype(jnp.float32)

def row_norm(values, scales):
    return values * lax.rsqrt(lax.optimization_barrier(jnp.mean(values * values, axis=-1, keepdims=True)) + EPSILON) * scales

def quarter_sum(lhs_rows, rhs_cols):
    column_span = lhs_rows.shape[1] // N_FFN
    running_sum = jnp.zeros((lhs_rows.shape[0], rhs_cols.shape[1]), jnp.float32)
    for quarter in range(N_FFN):
        partial_term = jnp.dot(lhs_rows[:, quarter * column_span:(quarter + 1) * column_span], rhs_cols[quarter * column_span:(quarter + 1) * column_span], preferred_element_type=jnp.float32)
        running_sum = running_sum + rounded(partial_term)
    return running_sum

def slot_positions(owner_ids):
    grouped = owner_ids.reshape(N_SEQ, TOK_DEV)
    matched = (grouped[:, :, None] == jnp.arange(N_SEQ, dtype=jnp.int32)[None, None, :]).astype(jnp.int32)
    within = lax.optimization_barrier(jnp.sum(matched * (jnp.cumsum(matched, axis=1) - 1), axis=2))
    sources = jnp.arange(N_SEQ, dtype=jnp.int32)[:, None]
    return (grouped * SLOT_DEV + sources * CAP + within).reshape(TOKENS).astype(jnp.int32)

def reference(child_feat, parent_feat, child_parent, owner, log_gate, norm_gain, w_query, w_key, w_value, head_gain, w_out, ffn_gain, w_up, w_down):
    parent_rows = jnp.arange(TOKENS, dtype=jnp.int32) // TOK_DEV * PAR_DEV + child_parent
    joined = (child_feat.astype(jnp.float32) + parent_feat.astype(jnp.float32)[parent_rows]).astype(jnp.bfloat16)
    slot_of = slot_positions(owner[:, 0])
    slots = jnp.zeros((SLOT_TOTAL, D), jnp.bfloat16).at[slot_of].set(joined)
    slot_blocks = slots.reshape(N_SEQ, SLOT_DEV, D)
    gate_blocks = log_gate.reshape(HEAD_TOTAL, N_SEQ, SLOT_DEV).transpose(1, 0, 2)
    head_scales = head_gain.astype(jnp.float32).reshape(HEAD_TOTAL, HD)

    def advance(carried, block_item):
        slot_rows, gate_logarithms = block_item
        span_rows = slot_rows.shape[0]
        residual_in = slot_rows.astype(jnp.float32)
        normed = row_norm(residual_in, norm_gain.astype(jnp.float32)).astype(jnp.bfloat16)
        queries = rounded(jnp.dot(normed, w_query, preferred_element_type=jnp.float32)).reshape(span_rows, HEAD_TOTAL, HD)
        key_rows = rounded(jnp.dot(normed, w_key, preferred_element_type=jnp.float32)).reshape(span_rows, HEAD_TOTAL, HD)
        value_rows = rounded(jnp.dot(normed, w_value, preferred_element_type=jnp.float32)).reshape(span_rows, HEAD_TOTAL, HD)
        running = jnp.cumsum(gate_logarithms, axis=1)
        position = jnp.arange(span_rows, dtype=jnp.int32)
        causal = (position[:, None] >= position[None, :])[None]
        spacing = running[:, :, None] - running[:, None, :]
        decay_mat = jnp.where(causal, jnp.exp(jnp.where(causal, spacing, 0.0)), 0.0)
        scores = jnp.einsum('shd,thd->hst', queries, key_rows)
        mixing = rounded(scores * decay_mat)
        inside = jnp.einsum('hst,thd->shd', mixing, value_rows)
        outside = jnp.exp(running).T[:, :, None] * jnp.einsum('shd,hde->she', queries, carried, precision=PRECISE)
        combined = inside + outside
        per_head = combined * lax.rsqrt(lax.optimization_barrier(jnp.mean(combined * combined, axis=-1, keepdims=True)) + EPSILON) * head_scales[None]
        flattened = per_head.astype(jnp.bfloat16).reshape(span_rows, HEAD_TOTAL * HD)
        hidden = residual_in + quarter_sum(flattened, w_out)
        second = row_norm(hidden, ffn_gain.astype(jnp.float32)).astype(jnp.bfloat16)
        expanded = jax.nn.gelu(jnp.dot(second, w_up, preferred_element_type=jnp.float32)).astype(jnp.bfloat16)
        refined = (hidden + quarter_sum(expanded, w_down)).astype(jnp.bfloat16)
        block_end = running[:, -1]
        fading = jnp.exp(block_end[:, None] - running).T
        new_state = jnp.exp(block_end)[:, None, None] * carried + jnp.einsum('shd,she->hde', key_rows * fading[:, :, None], value_rows, precision=PRECISE)
        return (new_state, refined)
    initial = jnp.zeros((HEAD_TOTAL, HD, HD), jnp.float32)
    _, outputs = lax.scan(advance, initial, (slot_blocks, gate_blocks))
    return outputs.reshape(SLOT_TOTAL, D)[slot_of]
```

```python
import functools

import jax
import jax.numpy as jnp
from jax import lax
from jax.experimental import pallas as pl
from jax.experimental.pallas import tpu as pltpu
from jax.sharding import PartitionSpec as P

EPSILON = 1e-05
F32 = jnp.float32
BF16 = jnp.bfloat16
LANES = 128
NT = (((1,), (1,)), ((), ()))
TN = (((0,), (0,)), ((), ()))
VMEM = pl.BlockSpec(memory_space=pltpu.VMEM)


def split3(values):
    high = values.astype(BF16)
    rest = values - high.astype(F32)
    middle = rest.astype(BF16)
    low = (rest - middle.astype(F32)).astype(BF16)
    return high, middle, low


def dot(a, b):
    return jnp.dot(a, b, preferred_element_type=F32)


def iota(shape, dim):
    return lax.broadcasted_iota(jnp.int32, shape, dim)


def row_norm(values, scales):
    return values * lax.rsqrt(jnp.mean(values * values, axis=-1, keepdims=True) + EPSILON) * scales


def column(row, width=LANES):
    return jnp.broadcast_to(row, (width, row.shape[1])).T


def head_of_lane(shape, hd):
    return iota(shape, len(shape) - 1) // hd


def pre_kernel(cap, blocks, cf, pf, pick, own, gain, wq, wk, wv, joined, q, k, v, taken):
    tokens = cf.shape[0]
    parents = pf.shape[0]
    tile = min(256, tokens)
    owners = own[...]
    lane = iota((1, blocks * cap), 1)
    lane_owner, lane_rank = lane // cap, lane % cap
    ones = jnp.ones((tokens, LANES), BF16)
    for at in range(0, tokens, tile):
        rows = pl.ds(at, tile)
        chosen = jnp.where(iota((parents, tile), 0) == pick[:, rows], 1.0, 0.0).astype(BF16)
        added = lax.dot_general(chosen, pf[...], TN, preferred_element_type=F32)
        summed = (cf[rows, :].astype(F32) + added).astype(BF16)
        joined[rows, :] = summed
        normed = row_norm(summed.astype(F32), gain[...].astype(F32)).astype(BF16)
        q[rows, :] = dot(normed, wq[...]).astype(BF16)
        k[rows, :] = dot(normed, wk[...]).astype(BF16)
        v[rows, :] = dot(normed, wv[...]).astype(BF16)
        mine = column(own[:, rows])
        same = (mine[:, :1] == owners) & (iota((tile, tokens), 0) + at >= iota((tile, tokens), 1))
        count = dot(jnp.where(same, 1.0, 0.0).astype(BF16), ones)
        rank = count[:, :1].astype(jnp.int32) - 1
        match = mine[:, :1] == lane_owner
        kept = match & (lane_rank <= rank)
        left = match & (lane_rank > rank)
        taken[rows, :] = jnp.where(kept, 1.0, 0.0).astype(BF16)
        taken[pl.ds(tokens + at, tile), :] = jnp.where(left, 1.0, 0.0).astype(BF16)


def gate_rows(gates, cap, blocks):
    if len(gates.shape) == 3:
        rows = jnp.concatenate([gates[o][:, :cap] for o in range(blocks)], axis=1)
    else:
        rows = gates[...]
    heads = rows.shape[0]
    rows = jnp.concatenate([rows, jnp.zeros((8 - heads, rows.shape[1]), F32)], axis=0)
    return jnp.concatenate([part.astype(F32) for part in split3(rows)], axis=0).astype(BF16)


def state_kernel(cap, blocks, hd, taken, gates, k, v, own, states, c_lanes):
    tokens, share = k.shape
    table = gate_rows(gates, cap, blocks)
    summed = lax.dot_general(taken[...], table, NT, preferred_element_type=F32)
    spread = jnp.where(
        iota((24, share), 0) % 8 == head_of_lane((24, share), hd), 1.0, 0.0
    ).astype(BF16)
    wide = sum(dot(part, spread) for part in split3(summed))
    c_lanes[...] = wide[:tokens]
    faded = k[...].astype(F32) * jnp.exp(wide[tokens:])
    turned = faded.astype(BF16).T
    owners = own[...]
    values = v[...]
    lane_head = head_of_lane((hd, share), hd)

    def one(o, nothing):
        masked = jnp.where(owners == o, turned, jnp.zeros_like(turned))
        full = dot(masked, values)
        packed = jnp.zeros((hd, share), F32)
        for h in range(share // hd):
            packed = jnp.where(lane_head == h, full[h * hd : (h + 1) * hd], packed)
        states[o] = packed.astype(BF16)
        return nothing

    lax.fori_loop(0, blocks, one, 0, unroll=blocks <= 8)


def combine_kernel(blocks, hd, states, decay, back):
    def step(b, carry):
        back[b, :hd, :] = carry.astype(BF16)
        return decay[pl.ds(b, 1), :] * carry + states[b].astype(F32)

    total = lax.fori_loop(
        0, blocks, step, jnp.zeros(states.shape[1:], F32), unroll=blocks <= 8
    ).astype(BF16)
    for b in range(blocks):
        back[b, hd:, :] = total


def inside_kernel(cap, blocks, hd, q, k, v, taken, gates, c_lanes, own, inside):
    tokens, share = q.shape
    heads = share // hd
    table = gate_rows(gates, cap, blocks)
    turned = lax.dot_general(table, taken[:tokens, :], NT, preferred_element_type=F32)
    c_rows = turned[:8] + turned[8:16] + turned[16:]
    tile = min(256, tokens)
    for at in range(0, tokens, tile):
        rows = pl.ds(at, tile)
        reach = at + tile
        mine = column(own[:, rows])[:, :1]
        same = (mine == own[:, :reach]) & (
            iota((tile, reach), 0) + at >= iota((tile, reach), 1)
        )
        queries = q[rows, :]
        keys = k[:reach, :]
        values = v[:reach, :]
        total = jnp.zeros((tile, share), F32)
        for h in range(heads):
            only = head_of_lane((tile, share), hd) == h
            scores = lax.dot_general(
                jnp.where(only, queries, jnp.zeros_like(queries)),
                keys,
                NT,
                preferred_element_type=F32,
            )
            gap = c_lanes[rows, h * hd : h * hd + 1] - c_rows[h : h + 1, :reach]
            decay = jnp.where(same, jnp.exp(jnp.where(same, gap, 0.0)), 0.0)
            mixing = (scores * decay).astype(BF16)
            only = head_of_lane((reach, share), hd) == h
            total += dot(mixing, jnp.where(only, values, jnp.zeros_like(values)))
        inside[rows, :] = total


def outside_kernel(blocks, hd, back, lead, whole, q, own, c_lanes, inside, gain, flat, wide, table):
    tokens, share = q.shape
    heads = share // hd
    mine = column(own[...])[:, :1]
    queries = q[...]
    block_diagonal = iota((share, share), 0) // hd == iota((share, share), 1) // hd

    def step(o, carry):
        state = back[o, :hd, :].astype(F32) + lead[pl.ds(o, 1), :] * carry
        stacked = jnp.concatenate([state] * heads, axis=0)
        at = pl.ds(pl.multiple_of(o * share, share), share)
        table[at, :] = jnp.where(block_diagonal, stacked, 0.0).astype(BF16)
        wide[:, at] = jnp.where(mine == o, queries, jnp.zeros_like(queries))
        return whole[pl.ds(o, 1), :] * carry + back[o, hd:, :].astype(F32)

    lax.fori_loop(0, blocks, step, jnp.zeros((hd, share), F32), unroll=blocks <= 8)
    outside = dot(wide[...], table[...]) * jnp.exp(c_lanes[...])
    combined = inside[...] + outside
    square = combined * combined
    mean = jnp.where(block_diagonal, 1.0 / hd, 0.0).astype(BF16)
    spread = sum(dot(part, mean) for part in split3(square))
    flat[...] = (combined * lax.rsqrt(spread + EPSILON) * gain[...].astype(F32)).astype(BF16)


def ffn_kernel(groups, index, *refs):
    flats, wouts = refs[:groups], refs[groups : 2 * groups]
    joined, gain, w_up, w_down, own, even, odd, scratch = refs[2 * groups :]
    mine = index[0]
    tokens, width = joined.shape
    cols = width // groups
    tile = min(256, tokens)
    for at in range(0, tokens, tile):
        rows = pl.ds(at, tile)
        hidden = joined[rows, :].astype(F32)
        for flat, wout in zip(flats, wouts):
            hidden = hidden + dot(flat[rows, :], wout[...])
        scratch[...] = hidden
        second = row_norm(hidden, gain[...].astype(F32)).astype(BF16)
        expanded = jax.nn.gelu(dot(second, w_up[...])).astype(BF16)
        for j in range(groups):
            target = pl.ds(pl.multiple_of((mine ^ j) * cols, cols), cols)
            piece = dot(expanded, w_down[:, target])
            half = pl.ds((j // 2) * cols, cols)
            if j == 0:
                own[rows, :] = piece + scratch[:, target]
            elif j % 2:
                odd[rows, half] = piece.astype(BF16)
            else:
                even[rows, pl.ds((j // 2 - 1) * cols, cols)] = piece


def flip(array, axis, bit):
    size = lax.axis_size(axis)
    return lax.ppermute(array, axis, [(i, i ^ bit) for i in range(size)])


def gather_flips(array, axis):
    size = lax.axis_size(axis)
    parts = {0: array}
    bit = size // 2
    while bit:
        for k in list(parts):
            parts[k ^ bit] = flip(parts[k], axis, bit)
        bit //= 2
    return [parts[k] for k in range(size)]


def shaped(shape, dtype):
    return jax.ShapeDtypeStruct(shape, dtype)


def exchange(array):
    return lax.all_to_all(array, "seq", split_axis=0, concat_axis=0, tiled=True)


def on_device(
    child_feat,
    parent_feat,
    child_parent,
    owner,
    log_gate,
    norm_gain,
    w_query,
    w_key,
    w_value,
    head_gain,
    w_out,
    ffn_gain,
    w_up,
    w_down,
):
    blocks = lax.axis_size("seq")
    groups = lax.axis_size("ffn")
    mine = lax.axis_index("ffn")
    block = lax.axis_index("seq")
    heads, slots = log_gate.shape
    cap = slots // blocks
    tokens, width = child_feat.shape
    share = w_query.shape[1]
    hd = share // heads
    cols = width // groups

    gates = log_gate.reshape(heads, blocks, cap)
    sums = jnp.sum(gates, axis=2)
    payload = jnp.concatenate(
        [gates.transpose(1, 0, 2), jnp.broadcast_to(sums[None], (blocks, heads, blocks))], axis=2
    )
    arrived = exchange(payload)
    all_sums = arrived[:, :, cap:]
    if cap % LANES:
        arrived = arrived[:, :, :cap].transpose(1, 0, 2).reshape(heads, slots)
    wout_parts = gather_flips(w_out, "ffn")

    own = owner.reshape(1, tokens)
    joined, q, k, v, taken = pl.pallas_call(
        functools.partial(pre_kernel, cap, blocks),
        out_shape=(
            shaped((tokens, width), BF16),
            shaped((tokens, share), BF16),
            shaped((tokens, share), BF16),
            shaped((tokens, share), BF16),
            shaped((2 * tokens, slots), BF16),
        ),
        in_specs=[VMEM] * 8,
        out_specs=[VMEM] * 5,
        name="pre",
    )(
        child_feat,
        parent_feat,
        child_parent.reshape(1, tokens),
        own,
        norm_gain.reshape(1, width),
        w_query,
        w_key,
        w_value,
    )

    states, c_lanes = pl.pallas_call(
        functools.partial(state_kernel, cap, blocks, hd),
        out_shape=(shaped((blocks, hd, share), BF16), shaped((tokens, share), F32)),
        in_specs=[VMEM] * 5,
        out_specs=[VMEM] * 2,
        name="state",
    )(taken, arrived, k, v, own)
    states = exchange(states)

    inside = pl.pallas_call(
        functools.partial(inside_kernel, cap, blocks, hd),
        out_shape=shaped((tokens, share), F32),
        in_specs=[VMEM] * 7,
        out_specs=VMEM,
        name="inside",
    )(q, k, v, taken, arrived, c_lanes, own)

    decay = jnp.repeat(jnp.exp(sums).T, hd, axis=1)
    back = pl.pallas_call(
        functools.partial(combine_kernel, blocks, hd),
        out_shape=shaped((blocks, 2 * hd, share), BF16),
        in_specs=[VMEM] * 2,
        out_specs=VMEM,
        name="combine",
    )(states, decay)
    back = exchange(back)

    before = jnp.arange(blocks, dtype=jnp.int32) < block
    lead = jnp.repeat(jnp.exp(jnp.sum(jnp.where(before, all_sums, 0.0), axis=2)), hd, axis=1)
    whole = jnp.repeat(jnp.exp(jnp.sum(all_sums, axis=2)), hd, axis=1)
    flat = pl.pallas_call(
        functools.partial(outside_kernel, blocks, hd),
        out_shape=shaped((tokens, share), BF16),
        in_specs=[VMEM] * 8,
        out_specs=VMEM,
        scratch_shapes=[
            pltpu.VMEM((tokens, blocks * share), BF16),
            pltpu.VMEM((blocks * share, share), BF16),
        ],
        name="outside",
    )(back, lead, whole, q, own, c_lanes, inside, head_gain.reshape(1, share))

    flat_parts = gather_flips(flat, "ffn")
    half = groups // 2
    kept, even, odd = pl.pallas_call(
        functools.partial(ffn_kernel, groups),
        out_shape=(
            shaped((tokens, cols), F32),
            shaped((tokens, max(half - 1, 1) * cols), F32),
            shaped((tokens, half * cols), BF16),
        ),
        in_specs=[pl.BlockSpec(memory_space=pltpu.SMEM)] + [VMEM] * (2 * groups + 4),
        out_specs=[VMEM] * 3,
        scratch_shapes=[pltpu.VMEM((min(256, tokens), width), F32)],
        name="ffn",
    )(
        mine.reshape(1).astype(jnp.int32),
        *flat_parts,
        *wout_parts,
        joined,
        ffn_gain.reshape(1, width),
        w_up,
        w_down,
    )
    near = flip(odd, "ffn", 1).astype(F32)
    pieces = {0: kept + near[:, :cols]}
    for j in range(2, groups, 2):
        at = j // 2 * cols
        pieces[j] = even[:, at - cols : at] + near[:, at : at + cols]
    bit = 2
    while bit < groups:
        for j in [j for j in pieces if j & bit]:
            pieces[j ^ bit] = pieces[j ^ bit] + flip(pieces.pop(j).astype(BF16), "ffn", bit).astype(F32)
        bit *= 2
    return pieces[0].astype(BF16)


def solution(mesh):
    in_specs = (
        P("seq", None),
        P("seq", None),
        P("seq"),
        P("seq", None),
        P("ffn", "seq"),
        P(),
        P(None, "ffn"),
        P(None, "ffn"),
        P(None, "ffn"),
        P("ffn"),
        P("ffn", None),
        P(),
        P(None, "ffn"),
        P("ffn", None),
    )
    return jax.shard_map(
        on_device, mesh=mesh, in_specs=in_specs, out_specs=P("seq", "ffn"), check_vma=False
    )
```

```python
import functools

import jax
import jax.numpy as jnp
from jax import lax
from jax.experimental import pallas as pl
from jax.experimental.pallas import tpu as pltpu
from jax.sharding import PartitionSpec as P


EPSILON = 1e-05
F32 = jnp.float32
BF16 = jnp.bfloat16
LANES = 128
NT = (((1,), (1,)), ((), ()))
TN = (((0,), (0,)), ((), ()))
VMEM = pl.BlockSpec(memory_space=pltpu.VMEM)
HBM = pl.BlockSpec(memory_space=pltpu.HBM)


def split3(values):
    high = values.astype(BF16)
    rest = values - high.astype(F32)
    middle = rest.astype(BF16)
    low = (rest - middle.astype(F32)).astype(BF16)
    return high, middle, low


def dot(a, b):
    return jnp.dot(a, b, preferred_element_type=F32)


def iota(shape, dim):
    return lax.broadcasted_iota(jnp.int32, shape, dim)


def row_norm(values, scales):
    return values * lax.rsqrt(jnp.mean(values * values, axis=-1, keepdims=True) + EPSILON) * scales


def column(row, width=LANES):
    return jnp.broadcast_to(row, (width, row.shape[1])).T


def head_of_lane(shape, hd):
    return iota(shape, len(shape) - 1) // hd


def fetch(pairs, sems):
    copies = [pltpu.make_async_copy(src, dst, sems.at[i]) for i, (src, dst) in enumerate(pairs)]
    for copy in copies:
        copy.start()
    return copies


def pre_kernel(
    cap, blocks, cf, pf, pick, own, gain, wq, wk, wv,
    joined, q, k, v, taken, own_out,
    cf_v, pf_v, pick_v, own_v, gain_v, w_v, joined_v, sems, out_sems,
):
    tokens = cf.shape[0]
    parents = pf.shape[0]
    tile = min(256, tokens)
    starts = range(0, tokens, tile)
    small = fetch(
        [(own, own_v), (pick, pick_v), (pf, pf_v), (gain, gain_v)]
        + [(cf.at[pl.ds(at, tile)], cf_v.at[pl.ds(at, tile)]) for at in starts]
        + [(w, w_v.at[i]) for i, w in enumerate((wq, wk, wv))],
        sems,
    )
    parts, weights = small[4 : 4 + len(starts)], small[4 + len(starts) :]
    small[0].wait()
    owners = own_v[...]
    own_out[...] = owners
    lane = iota((1, blocks * cap), 1)
    lane_owner, lane_rank = lane // cap, lane % cap
    ones = jnp.ones((tokens, LANES), BF16)
    for at in starts:
        rows = pl.ds(at, tile)
        mine = column(own_v[:, rows])
        same = (mine[:, :1] == owners) & (iota((tile, tokens), 0) + at >= iota((tile, tokens), 1))
        count = dot(jnp.where(same, 1.0, 0.0).astype(BF16), ones)
        rank = count[:, :1].astype(jnp.int32) - 1
        kept = (mine[:, :1] == lane_owner) & (lane_rank <= rank)
        taken[rows, :] = jnp.where(kept, 1.0, 0.0).astype(BF16)
    for copy in small[1:4]:
        copy.wait()
    scales = gain_v[...].astype(F32).reshape(1, -1)
    stores = []
    for i, at in enumerate(starts):
        rows = pl.ds(at, tile)
        parts[i].wait()
        chosen = jnp.where(iota((parents, tile), 0) == pick_v[:, rows], 1.0, 0.0).astype(BF16)
        added = lax.dot_general(chosen, pf_v[...], TN, preferred_element_type=F32)
        summed = (cf_v[rows, :].astype(F32) + added).astype(BF16)
        joined_v[rows, :] = summed
        store = pltpu.make_async_copy(joined_v.at[rows], joined.at[rows], out_sems.at[i])
        store.start()
        stores.append(store)
        normed = row_norm(summed.astype(F32), scales).astype(BF16)
        if i == 0:
            for copy in weights:
                copy.wait()
        for j, out in enumerate((q, k, v)):
            out[rows, :] = dot(normed, w_v[j]).astype(BF16)
    for store in stores:
        store.wait()


def gate_rows(gates, blocks):
    if len(gates.shape) == 3:
        rows = jnp.concatenate([gates[o] for o in range(blocks)], axis=1)
    else:
        rows = gates[...]
    heads = rows.shape[0]
    rows = jnp.concatenate([rows, jnp.zeros((8 - heads, rows.shape[1]), F32)], axis=0)
    return jnp.concatenate([part.astype(F32) for part in split3(rows)], axis=0).astype(BF16)


def state_kernel(cap, blocks, hd, taken, gates, k, v, own, states, c_lanes, c_rows, states_v, sems):
    tokens, share = k.shape
    table = gate_rows(gates, blocks)
    summed = lax.dot_general(taken[...], table, NT, preferred_element_type=F32)
    slots = table.shape[1]
    lanes = LANES * pl.cdiv(blocks, LANES)
    chunk = jnp.where(
        iota((slots, lanes), 0) // cap == iota((slots, lanes), 1), 1.0, 0.0
    ).astype(BF16)
    totals = dot(table, chunk)
    totals = jnp.concatenate(
        [part.astype(F32) for part in split3(totals[:8] + totals[8:16] + totals[16:])], axis=0
    ).astype(BF16)
    named = jnp.where(column(own[...])[:, :1] == iota((tokens, lanes), 1), 1.0, 0.0).astype(BF16)
    whole = lax.dot_general(named, totals, NT, preferred_element_type=F32)
    summed = jnp.concatenate([summed, whole], axis=0)
    spread = jnp.where(
        iota((24, share), 0) % 8 == head_of_lane((24, share), hd), 1.0, 0.0
    ).astype(BF16)
    wide = sum(dot(part, spread) for part in split3(summed))
    c_lanes[...] = wide[:tokens]
    turned_c = lax.dot_general(table, taken[...], NT, preferred_element_type=F32)
    c_rows[...] = turned_c[:8] + turned_c[8:16] + turned_c[16:]
    faded = k[...].astype(F32) * jnp.exp(jnp.minimum(wide[tokens:] - wide[:tokens], 0.0))
    turned = faded.astype(BF16).T
    owners = own[...]
    values = v[...]
    lane_head = head_of_lane((hd, share), hd)

    def one(o, nothing):
        masked = jnp.where(owners == o, turned, jnp.zeros_like(turned))
        full = dot(masked, values)
        packed = jnp.zeros((hd, share), F32)
        for h in range(share // hd):
            packed = jnp.where(lane_head == h, full[h * hd : (h + 1) * hd], packed)
        states_v[o] = packed.astype(BF16)
        pltpu.make_async_copy(states_v.at[o], states.at[o], sems.at[o]).start()
        return nothing

    lax.fori_loop(0, blocks, one, 0, unroll=blocks <= 8)
    for o in range(blocks):
        pltpu.make_async_copy(states_v.at[o], states.at[o], sems.at[o]).wait()


def decay_kernel(cap, blocks, hd, gates, decay, tail, gates_v, sem):
    fetch([(gates, gates_v)], sem)[0].wait()
    slots = gates.shape[1]
    share = decay.shape[1]
    table = gate_rows(gates_v, blocks)
    rows = 8 * pl.cdiv(blocks, 8)
    lane_chunk = iota((rows, slots), 1) // cap
    chunk = iota((rows, slots), 0)
    picked = [lane_chunk == chunk, lane_chunk < chunk, lane_chunk >= 0]
    spread = jnp.where(
        iota((24, share), 0) % 8 == head_of_lane((24, share), hd), 1.0, 0.0
    ).astype(BF16)
    outs = []
    for mask in picked:
        summed = lax.dot_general(
            jnp.where(mask, 1.0, 0.0).astype(BF16), table, NT, preferred_element_type=F32
        )
        outs.append(jnp.exp(sum(dot(part, spread) for part in split3(summed))))
    decay[...] = outs[0]
    for at, value in ((0, outs[1]), (4, outs[2])):
        for i, part in enumerate(split3(value)):
            for b in range(blocks):
                tail[b, at + i : at + i + 1, :] = part[b : b + 1].astype(F32)
    for at in (3, 7):
        for b in range(blocks):
            tail[b, at : at + 1, :] = jnp.zeros((1, share), F32)


def combine_kernel(blocks, hd, states, decay, tail, ordered, back):
    def step(b, carry):
        back[b, :hd, :] = carry.astype(BF16)
        back[b, 2 * hd :, :] = tail[b].astype(BF16)
        return decay[pl.ds(b, 1), :] * carry + states[b].astype(F32)

    total = lax.fori_loop(
        0, blocks, step, jnp.zeros(states.shape[1:], F32), unroll=blocks <= 8
    ).astype(BF16)
    for b in range(blocks):
        back[b, hd : 2 * hd, :] = total


def inside_kernel(hd, q, k, v, c_lanes, c_rows, own, inside):
    tokens, share = q.shape
    heads = share // hd
    tile = min(256, tokens)
    for at in range(0, tokens, tile):
        rows = pl.ds(at, tile)
        reach = at + tile
        mine = column(own[:, rows])[:, :1]
        same = (mine == own[:, :reach]) & (
            iota((tile, reach), 0) + at >= iota((tile, reach), 1)
        )
        queries = q[rows, :]
        keys = k[:reach, :]
        values = v[:reach, :]
        total = jnp.zeros((tile, share), F32)
        for h in range(heads):
            only = head_of_lane((tile, share), hd) == h
            scores = lax.dot_general(
                jnp.where(only, queries, jnp.zeros_like(queries)),
                keys,
                NT,
                preferred_element_type=F32,
            )
            gap = c_lanes[rows, h * hd : h * hd + 1] - c_rows[h : h + 1, :reach]
            decay = jnp.where(same, jnp.exp(jnp.where(same, gap, 0.0)), 0.0)
            mixing = (scores * decay).astype(BF16)
            only = head_of_lane((reach, share), hd) == h
            total += dot(mixing, jnp.where(only, values, jnp.zeros_like(values)))
        inside[rows, :] = total


def outside_kernel(blocks, hd, back, q, own, c_lanes, inside, gain, first, second, wide, table):
    tokens, share = q.shape
    heads = share // hd
    mine = column(own[...])[:, :1]
    queries = q[...]
    block_diagonal = iota((share, share), 0) // hd == iota((share, share), 1) // hd

    def step(o, carry):
        tail = back[o, 2 * hd :, :].astype(F32)
        lead = tail[0:1] + tail[1:2] + tail[2:3]
        whole = tail[4:5] + tail[5:6] + tail[6:7]
        state = back[o, :hd, :].astype(F32) + lead * carry
        stacked = jnp.concatenate([state] * heads, axis=0)
        at = pl.ds(pl.multiple_of(o * share, share), share)
        table[at, :] = jnp.where(block_diagonal, stacked, 0.0).astype(BF16)
        wide[:, at] = jnp.where(mine == o, queries, jnp.zeros_like(queries))
        return whole * carry + back[o, hd : 2 * hd, :].astype(F32)

    lax.fori_loop(0, blocks, step, jnp.zeros((hd, share), F32), unroll=blocks <= 8)
    outside = dot(wide[...], table[...]) * jnp.exp(c_lanes[...])
    combined = inside[...] + outside
    square = combined * combined
    mean = jnp.where(block_diagonal, 1.0 / hd, 0.0).astype(BF16)
    spread = sum(dot(part, mean) for part in split3(square))
    flat = (combined * lax.rsqrt(spread + EPSILON) * gain[...].astype(F32)).astype(BF16)
    first[...] = flat[: tokens // 2]
    second[...] = flat[tokens // 2 :]


def load_kernel(groups, *refs):
    owns, nears, wouts = refs[0:2], refs[2:4], refs[4 : 4 + groups]
    joined, gain, w_up, w_down = refs[4 + groups : 8 + groups]
    hidden, wout_v, scale, up_v, down_v = refs[8 + groups : 13 + groups]
    joined_v, gain_v, near_v, sems = refs[13 + groups :]
    copies = fetch(
        [(wouts[0], near_v.at[0]), (wouts[1], near_v.at[1]), (joined, joined_v), (gain, gain_v)]
        + [(w, wout_v.at[i]) for i, w in enumerate(wouts[2:])]
        + [(w_up, up_v), (w_down, down_v)],
        sems,
    )
    for copy in copies[:4]:
        copy.wait()
    scale[...] = gain_v[...].astype(F32).reshape(1, -1)
    rows = owns[0].shape[0]
    for i in range(2):
        at = pl.ds(i * rows, rows)
        hidden[at, :] = (
            joined_v[at, :].astype(F32)
            + dot(owns[i][...], near_v[0])
            + dot(nears[i][...], near_v[1])
        )
    for copy in copies[4:]:
        copy.wait()


def ffn_kernel(groups, at, *refs):
    flats = refs[: groups - 2]
    hidden_v, wout_v, scale, up_v, down_v, own, even, odd, scratch = refs[groups - 2 :]
    mine = lax.axis_index("ffn")
    rows, cols = own.shape
    hidden = hidden_v[pl.ds(at, rows), :]
    for i, flat in enumerate(flats):
        hidden = hidden + dot(flat[...], wout_v[i])
    scratch[...] = hidden
    second = row_norm(hidden, scale[...]).astype(BF16)
    expanded = jax.nn.gelu(dot(second, up_v[...])).astype(BF16)
    for j in sorted(range(groups), key=lambda j: -(j % 2)):
        target = pl.ds(pl.multiple_of((mine ^ j) * cols, cols), cols)
        piece = dot(expanded, down_v[:, target])
        if j == 0:
            own[...] = piece + scratch[:, target]
        elif j % 2:
            odd[:, pl.ds((j // 2) * cols, cols)] = piece.astype(BF16)
        else:
            even[:, pl.ds((j // 2 - 1) * cols, cols)] = piece


def final_kernel(*refs):
    out = refs[-1]
    for i in range(2):
        own, near, far = refs[3 * i : 3 * i + 3]
        rows, cols = own.shape
        out[pl.ds(i * rows, rows), :] = (
            own[...] + near[:, :cols].astype(F32) + far[...].astype(F32)
        ).astype(BF16)


def flip(array, axis, bit):
    size = lax.axis_size(axis)
    return lax.ppermute(array, axis, [(i, i ^ bit) for i in range(size)])


def gather_flips(array, axis):
    size = lax.axis_size(axis)
    parts = {0: array}
    bit = size // 2
    while bit:
        for k in list(parts):
            parts[k ^ bit] = flip(parts[k], axis, bit)
        bit //= 2
    return [parts[k] for k in range(size)]


def grant(mebibytes):
    return pltpu.CompilerParams(vmem_limit_bytes=mebibytes << 20)


def shaped(shape, dtype):
    return jax.ShapeDtypeStruct(shape, dtype)


def in_hbm(array):
    return pltpu.with_memory_space_constraint(array, pltpu.HBM)


def exchange(array):
    return lax.all_to_all(array, "seq", split_axis=0, concat_axis=0, tiled=True)


def on_device(
    child_feat,
    parent_feat,
    child_parent,
    owner,
    log_gate,
    norm_gain,
    w_query,
    w_key,
    w_value,
    head_gain,
    w_out,
    ffn_gain,
    w_up,
    w_down,
):
    blocks = lax.axis_size("seq")
    groups = lax.axis_size("ffn")
    heads, slots = log_gate.shape
    cap = slots // blocks
    tokens, width = child_feat.shape
    share = w_query.shape[1]
    hd = share // heads
    cols = width // groups

    child_feat, parent_feat, w_query, w_key, w_value, w_up, w_down = map(
        in_hbm, (child_feat, parent_feat, w_query, w_key, w_value, w_up, w_down)
    )
    arrived = exchange(log_gate.reshape(heads, blocks, cap).transpose(1, 0, 2))
    if cap % LANES:
        arrived = arrived.transpose(1, 0, 2).reshape(heads, slots)
    wout_parts = [in_hbm(part) for part in gather_flips(w_out, "ffn")]

    tiles = pl.cdiv(tokens, min(256, tokens))
    joined, q, k, v, taken, own = pl.pallas_call(
        functools.partial(pre_kernel, cap, blocks),
        out_shape=(
            pltpu.HBM((tokens, width), BF16),
            shaped((tokens, share), BF16),
            shaped((tokens, share), BF16),
            shaped((tokens, share), BF16),
            shaped((tokens, slots), BF16),
            shaped((1, tokens), jnp.int32),
        ),
        in_specs=[HBM] * 8,
        out_specs=[HBM] + [VMEM] * 5,
        scratch_shapes=[
            pltpu.VMEM((tokens, width), BF16),
            pltpu.VMEM(parent_feat.shape, BF16),
            pltpu.VMEM((1, tokens), jnp.int32),
            pltpu.VMEM((1, tokens), jnp.int32),
            pltpu.VMEM((width,), BF16),
            pltpu.VMEM((3, width, share), BF16),
            pltpu.VMEM((tokens, width), BF16),
            pltpu.SemaphoreType.DMA((7 + tiles,)),
            pltpu.SemaphoreType.DMA((tiles,)),
        ],
        name="pre",
        compiler_params=grant(20),
    )(
        child_feat,
        parent_feat,
        in_hbm(child_parent.reshape(1, tokens)),
        in_hbm(owner.reshape(1, tokens)),
        in_hbm(norm_gain),
        w_query,
        w_key,
        w_value,
    )

    states, c_lanes, c_rows = pl.pallas_call(
        functools.partial(state_kernel, cap, blocks, hd),
        out_shape=(
            pltpu.HBM((blocks, hd, share), BF16),
            shaped((tokens, share), F32),
            shaped((8, tokens), F32),
        ),
        in_specs=[VMEM] * 5,
        out_specs=[HBM] + [VMEM] * 2,
        scratch_shapes=[
            pltpu.VMEM((blocks, hd, share), BF16),
            pltpu.SemaphoreType.DMA((blocks,)),
        ],
        name="state",
        compiler_params=grant(12),
    )(taken, arrived, k, v, own)
    states = exchange(states)

    inside = pl.pallas_call(
        functools.partial(inside_kernel, hd),
        out_shape=shaped((tokens, share), F32),
        in_specs=[VMEM] * 6,
        out_specs=VMEM,
        name="inside",
        compiler_params=grant(12),
    )(q, k, v, c_lanes, c_rows, own)

    decay, tail = pl.pallas_call(
        functools.partial(decay_kernel, cap, blocks, hd),
        out_shape=(
            shaped((8 * pl.cdiv(blocks, 8), share), F32),
            shaped((blocks, 8, share), F32),
        ),
        in_specs=[HBM],
        out_specs=[VMEM] * 2,
        scratch_shapes=[pltpu.VMEM((heads, slots), F32), pltpu.SemaphoreType.DMA((1,))],
        name="decay",
        compiler_params=grant(8),
    )(log_gate)

    back = pl.pallas_call(
        functools.partial(combine_kernel, blocks, hd),
        out_shape=shaped((blocks, 2 * hd + 8, share), BF16),
        in_specs=[VMEM] * 4,
        out_specs=VMEM,
        name="combine",
        compiler_params=grant(8),
    )(states, decay, tail, inside)
    back = exchange(back)

    flats = pl.pallas_call(
        functools.partial(outside_kernel, blocks, hd),
        out_shape=(shaped((tokens // 2, share), BF16),) * 2,
        in_specs=[VMEM] * 6,
        out_specs=[VMEM] * 2,
        scratch_shapes=[
            pltpu.VMEM((tokens, blocks * share), BF16),
            pltpu.VMEM((blocks * share, share), BF16),
        ],
        name="outside",
        compiler_params=grant(16 if blocks <= 8 else 48),
    )(back, q, own, c_lanes, inside, head_gain.reshape(1, share))

    rows, half = tokens // 2, groups // 2
    parts = [gather_flips(flat, "ffn") for flat in flats]
    load = pl.pallas_call(
        functools.partial(load_kernel, groups),
        out_shape=(
            pltpu.VMEM((tokens, width), F32),
            pltpu.VMEM((groups - 2, share, width), BF16),
            pltpu.VMEM((1, width), F32),
            pltpu.VMEM(w_up.shape, BF16),
            pltpu.VMEM(w_down.shape, BF16),
        ),
        in_specs=[VMEM] * 4 + [HBM] * (groups + 4),
        out_specs=[VMEM] * 5,
        scratch_shapes=[
            pltpu.VMEM((tokens, width), BF16),
            pltpu.VMEM((width,), BF16),
            pltpu.VMEM((2, share, width), BF16),
            pltpu.SemaphoreType.DMA((groups + 4,)),
        ],
        name="load",
        compiler_params=grant(12),
    )
    loaded = load(
        parts[0][0],
        parts[1][0],
        parts[0][1],
        parts[1][1],
        *wout_parts,
        in_hbm(joined),
        in_hbm(ffn_gain),
        w_up,
        w_down,
    )
    finals = []
    for i in range(2):
        kept, even, odd = pl.pallas_call(
            functools.partial(ffn_kernel, groups, i * rows),
            out_shape=(
                shaped((rows, cols), F32),
                shaped((rows, max(half - 1, 1) * cols), F32),
                shaped((rows, half * cols), BF16),
            ),
            in_specs=[VMEM] * (groups + 3),
            out_specs=[VMEM] * 3,
            scratch_shapes=[pltpu.VMEM((rows, width), F32)],
            compiler_params=grant(12),
        )(*parts[i][2:], *loaded)
        near = flip(odd, "ffn", 1)
        pieces = {
            j: (
                even[:, (j // 2 - 1) * cols : j // 2 * cols]
                + near[:, j // 2 * cols : (j // 2 + 1) * cols].astype(F32)
            )
            for j in range(2, groups, 2)
        }
        far = [flip(pieces[j].astype(BF16), "ffn", j) for j in pieces]
        far = far[0] if len(far) == 1 else sum(part.astype(F32) for part in far)
        finals += [kept, near, far]
    return pl.pallas_call(
        final_kernel,
        out_shape=shaped((tokens, cols), BF16),
        in_specs=[VMEM] * 6,
        out_specs=VMEM,
        name="final",
        compiler_params=grant(8),
    )(*finals)


def solution(mesh):
    in_specs = (
        P("seq", None),
        P("seq", None),
        P("seq"),
        P("seq", None),
        P("ffn", "seq"),
        P(),
        P(None, "ffn"),
        P(None, "ffn"),
        P(None, "ffn"),
        P("ffn"),
        P("ffn", None),
        P(),
        P(None, "ffn"),
        P("ffn", None),
    )

    return jax.shard_map(
        on_device, mesh=mesh, in_specs=in_specs, out_specs=P("seq", "ffn"), check_vma=False
    )
```

```python
import functools

import jax
import jax.numpy as jnp
from jax import lax
from jax.experimental import pallas as pl
from jax.experimental.pallas import tpu as pltpu
from jax.sharding import PartitionSpec as P


EPSILON = 1e-05
F32 = jnp.float32
BF16 = jnp.bfloat16
LANES = 128
NT = (((1,), (1,)), ((), ()))
TN = (((0,), (0,)), ((), ()))
VMEM = pl.BlockSpec(memory_space=pltpu.VMEM)
HBM = pl.BlockSpec(memory_space=pltpu.HBM)


def split3(values):
    high = values.astype(BF16)
    rest = values - high.astype(F32)
    middle = rest.astype(BF16)
    low = (rest - middle.astype(F32)).astype(BF16)
    return high, middle, low


def dot(a, b):
    return jnp.dot(a, b, preferred_element_type=F32)


def iota(shape, dim):
    return lax.broadcasted_iota(jnp.int32, shape, dim)


def row_norm(values, scales):
    return values * lax.rsqrt(jnp.mean(values * values, axis=-1, keepdims=True) + EPSILON) * scales


def column(row, width=LANES):
    return jnp.broadcast_to(row, (width, row.shape[1])).T


def head_of_lane(shape, hd):
    return iota(shape, len(shape) - 1) // hd


def fetch(pairs, sems):
    copies = [pltpu.make_async_copy(src, dst, sems.at[i]) for i, (src, dst) in enumerate(pairs)]
    for copy in copies:
        copy.start()
    return copies


def pre_kernel(
    cap, blocks, cf, pf, pick, own, gain, wq, wk, wv,
    joined, q, k, v, taken, own_out,
    cf_v, pf_v, pick_v, own_v, gain_v, w_v, joined_v, sems, out_sems,
):
    tokens = cf.shape[0]
    parents = pf.shape[0]
    tile = min(256, tokens)
    starts = range(0, tokens, tile)
    small = fetch(
        [(own, own_v), (pick, pick_v), (pf, pf_v), (gain, gain_v)]
        + [(cf.at[pl.ds(at, tile)], cf_v.at[pl.ds(at, tile)]) for at in starts]
        + [(w, w_v.at[i]) for i, w in enumerate((wq, wk, wv))],
        sems,
    )
    parts, weights = small[4 : 4 + len(starts)], small[4 + len(starts) :]
    small[0].wait()
    owners = own_v[...]
    own_out[...] = owners
    lane = iota((1, blocks * cap), 1)
    lane_owner, lane_rank = lane // cap, lane % cap
    ones = jnp.ones((tokens, LANES), BF16)
    for at in starts:
        rows = pl.ds(at, tile)
        mine = column(own_v[:, rows])
        same = (mine[:, :1] == owners) & (iota((tile, tokens), 0) + at >= iota((tile, tokens), 1))
        count = dot(jnp.where(same, 1.0, 0.0).astype(BF16), ones)
        rank = count[:, :1].astype(jnp.int32) - 1
        kept = (mine[:, :1] == lane_owner) & (lane_rank <= rank)
        taken[rows, :] = jnp.where(kept, 1.0, 0.0).astype(BF16)
    for copy in small[1:4]:
        copy.wait()
    scales = gain_v[...].astype(F32).reshape(1, -1)
    stores = []
    for i, at in enumerate(starts):
        rows = pl.ds(at, tile)
        parts[i].wait()
        chosen = jnp.where(iota((parents, tile), 0) == pick_v[:, rows], 1.0, 0.0).astype(BF16)
        added = lax.dot_general(chosen, pf_v[...], TN, preferred_element_type=F32)
        summed = (cf_v[rows, :].astype(F32) + added).astype(BF16)
        joined_v[rows, :] = summed
        store = pltpu.make_async_copy(joined_v.at[rows], joined.at[rows], out_sems.at[i])
        store.start()
        stores.append(store)
        normed = row_norm(summed.astype(F32), scales).astype(BF16)
        if i == 0:
            for copy in weights:
                copy.wait()
        for j, out in enumerate((q, k, v)):
            out[rows, :] = dot(normed, w_v[j]).astype(BF16)
    for store in stores:
        store.wait()


def gate_rows(gates, blocks):
    if len(gates.shape) == 3:
        rows = jnp.concatenate([gates[o] for o in range(blocks)], axis=1)
    else:
        rows = gates[...]
    heads = rows.shape[0]
    rows = jnp.concatenate([rows, jnp.zeros((8 - heads, rows.shape[1]), F32)], axis=0)
    return jnp.concatenate([part.astype(F32) for part in split3(rows)], axis=0).astype(BF16)


def seat(owner, blocks):
    half = max(blocks // 2, 1)
    return owner // half * (8 * pl.cdiv(half, 8)) + owner % half


def put_tail(send, decay, at):
    high = decay.astype(BF16)
    low = decay - high.astype(F32)
    send[at:, :] = jnp.concatenate([high.astype(F32), low], axis=0).astype(BF16)


def state_kernel(cap, blocks, hd, taken, gates, k, v, own, c_lanes, c_rows, *outs):
    tokens, share = k.shape
    half = blocks // 2
    rows = 8 * pl.cdiv(half, 8)
    table = gate_rows(gates, blocks)
    slots = table.shape[1]
    summed = lax.dot_general(taken[...], table, NT, preferred_element_type=F32)
    lanes = LANES * pl.cdiv(2 * rows, LANES)
    chunk = jnp.where(
        seat(iota((slots, lanes), 0) // cap, blocks) == iota((slots, lanes), 1), 1.0, 0.0
    ).astype(BF16)
    totals = dot(table, chunk)
    totals = jnp.concatenate(
        [part.astype(F32) for part in split3(totals[:8] + totals[8:16] + totals[16:])], axis=0
    ).astype(BF16)
    mine = column(seat(own[...], blocks))[:, :1]
    named = jnp.where(mine == iota((tokens, lanes), 1), 1.0, 0.0).astype(BF16)
    whole = lax.dot_general(named, totals, NT, preferred_element_type=F32)
    summed = jnp.concatenate([summed, whole], axis=0)
    spread = jnp.where(
        iota((24, share), 0) % 8 == head_of_lane((24, share), hd), 1.0, 0.0
    ).astype(BF16)
    wide = sum(dot(part, spread) for part in split3(summed))
    c_lanes[...] = wide[:tokens]
    turned_c = lax.dot_general(table, taken[...], NT, preferred_element_type=F32)
    c_rows[...] = turned_c[:8] + turned_c[8:16] + turned_c[16:]
    faded = k[...].astype(F32) * jnp.exp(jnp.minimum(wide[tokens:] - wide[:tokens], 0.0))
    turned = faded.astype(BF16).T
    decays = jnp.exp(lax.dot_general(totals, spread, TN, preferred_element_type=F32))
    owners = own[...]
    values = v[...]
    lane_head = head_of_lane((hd, share), hd)
    for g in range(2):
        send, state, decay = outs[3 * g : 3 * g + 3]

        def one(i, nothing):
            masked = jnp.where(owners == i + g * half, turned, jnp.zeros_like(turned))
            full = dot(masked, values)
            packed = jnp.zeros((hd, share), F32)
            for h in range(share // hd):
                packed = jnp.where(lane_head == h, full[h * hd : (h + 1) * hd], packed)
            state[i] = packed
            send[pl.ds(pl.multiple_of(i * hd, hd), hd), :] = packed.astype(BF16)
            return nothing

        lax.fori_loop(0, half, one, 0, unroll=blocks <= 8)
        decay[...] = decays[g * rows : (g + 1) * rows]
        put_tail(send, decay[...], half * hd)


def joined_scan(bit, hd, refs):
    came, state, decay, prefix, lead = refs
    half = state.shape[0]
    rows = decay.shape[0]
    upper = ((lax.axis_index("seq") & bit) // bit).astype(F32)
    tail = came[half * hd :, :].astype(F32)
    theirs_decay = tail[:rows] + tail[rows:]
    mine_decay = decay[...]
    past = jnp.ones_like(mine_decay) if lead is None else lead[...]
    scale_mine = upper + (1.0 - upper) * theirs_decay
    scale_theirs = upper * mine_decay + (1.0 - upper)
    add = upper * past
    pairs = []
    for i in range(half):
        theirs = came[i * hd : (i + 1) * hd, :].astype(F32)
        total = scale_mine[i : i + 1] * state[i] + scale_theirs[i : i + 1] * theirs
        before = add[i : i + 1] * theirs
        pairs.append((total, before if prefix is None else prefix[i] + before))
    return pairs, mine_decay * theirs_decay, past * scale_mine_lead(upper, theirs_decay)


def scale_mine_lead(upper, theirs_decay):
    return upper * theirs_decay + (1.0 - upper)


def step_kernel(bit, hd, first, *refs):
    came, state, decay = refs[:3]
    prefix, lead = (None, None) if first else refs[3:5]
    send, state_out, decay_out, prefix_out, lead_out = refs[-5:]
    pairs, total_decay, total_lead = joined_scan(bit, hd, (came, state, decay, prefix, lead))
    for i, (total, before) in enumerate(pairs):
        state_out[i] = total
        prefix_out[i] = before
        send[i * hd : (i + 1) * hd, :] = total.astype(BF16)
    decay_out[...] = total_decay
    lead_out[...] = total_lead
    put_tail(send, total_decay, len(pairs) * hd)


def inside_kernel(hd, q, k, v, c_lanes, c_rows, own, inside):
    tokens, share = q.shape
    heads = share // hd
    tile = min(256, tokens)
    for at in range(0, tokens, tile):
        rows = pl.ds(at, tile)
        reach = at + tile
        mine = column(own[:, rows])[:, :1]
        same = (mine == own[:, :reach]) & (
            iota((tile, reach), 0) + at >= iota((tile, reach), 1)
        )
        queries = q[rows, :]
        keys = k[:reach, :]
        values = v[:reach, :]
        total = jnp.zeros((tile, share), F32)
        for h in range(heads):
            only = head_of_lane((tile, share), hd) == h
            scores = lax.dot_general(
                jnp.where(only, queries, jnp.zeros_like(queries)),
                keys,
                NT,
                preferred_element_type=F32,
            )
            gap = c_lanes[rows, h * hd : h * hd + 1] - c_rows[h : h + 1, :reach]
            decay = jnp.where(same, jnp.exp(jnp.where(same, gap, 0.0)), 0.0)
            mixing = (scores * decay).astype(BF16)
            only = head_of_lane((reach, share), hd) == h
            total += dot(mixing, jnp.where(only, values, jnp.zeros_like(values)))
        inside[rows, :] = total


def outside_kernel(bit, hd, *refs):
    halves = [refs[5 * g : 5 * g + 5] for g in range(2)]
    q, own, c_lanes, inside, gain, first, second, wide, table = refs[10:]
    tokens, share = q.shape
    heads = share // hd
    mine = column(own[...])[:, :1]
    queries = q[...]
    block_diagonal = iota((share, share), 0) // hd == iota((share, share), 1) // hd
    carry = jnp.zeros((hd, share), F32)
    for g in range(2):
        pairs, whole, lead = joined_scan(bit, hd, halves[g])
        for i, (total, before) in enumerate(pairs):
            o = g * len(pairs) + i
            state = before + lead[i : i + 1] * carry
            stacked = jnp.concatenate([state] * heads, axis=0)
            at = pl.ds(o * share, share)
            table[at, :] = jnp.where(block_diagonal, stacked, 0.0).astype(BF16)
            wide[:, at] = jnp.where(mine == o, queries, jnp.zeros_like(queries))
            carry = whole[i : i + 1] * carry + total
    outside = dot(wide[...], table[...]) * jnp.exp(c_lanes[...])
    combined = inside[...] + outside
    square = combined * combined
    mean = jnp.where(block_diagonal, 1.0 / hd, 0.0).astype(BF16)
    spread = sum(dot(part, mean) for part in split3(square))
    flat = (combined * lax.rsqrt(spread + EPSILON) * gain[...].astype(F32)).astype(BF16)
    first[...] = flat[: tokens // 2]
    second[...] = flat[tokens // 2 :]


def load_kernel(groups, *refs):
    owns, nears, wouts = refs[0:2], refs[2:4], refs[4 : 4 + groups]
    joined, gain, w_up, w_down = refs[4 + groups : 8 + groups]
    hidden, wout_v, scale, up_v, down_v = refs[8 + groups : 13 + groups]
    joined_v, gain_v, near_v, sems = refs[13 + groups :]
    copies = fetch(
        [(wouts[0], near_v.at[0]), (wouts[1], near_v.at[1]), (joined, joined_v), (gain, gain_v)]
        + [(w, wout_v.at[i]) for i, w in enumerate(wouts[2:])]
        + [(w_up, up_v), (w_down, down_v)],
        sems,
    )
    for copy in copies[:4]:
        copy.wait()
    scale[...] = gain_v[...].astype(F32).reshape(1, -1)
    rows = owns[0].shape[0]
    for i in range(2):
        at = pl.ds(i * rows, rows)
        hidden[at, :] = (
            joined_v[at, :].astype(F32)
            + dot(owns[i][...], near_v[0])
            + dot(nears[i][...], near_v[1])
        )
    for copy in copies[4:]:
        copy.wait()


def ffn_kernel(groups, at, *refs):
    flats = refs[: groups - 2]
    hidden_v, wout_v, scale, up_v, down_v, own, even, odd, scratch = refs[groups - 2 :]
    mine = lax.axis_index("ffn")
    rows, cols = own.shape
    hidden = hidden_v[pl.ds(at, rows), :]
    for i, flat in enumerate(flats):
        hidden = hidden + dot(flat[...], wout_v[i])
    scratch[...] = hidden
    second = row_norm(hidden, scale[...]).astype(BF16)
    expanded = jax.nn.gelu(dot(second, up_v[...])).astype(BF16)
    for j in sorted(range(groups), key=lambda j: -(j % 2)):
        target = pl.ds(pl.multiple_of((mine ^ j) * cols, cols), cols)
        piece = dot(expanded, down_v[:, target])
        if j == 0:
            own[...] = piece + scratch[:, target]
        elif j % 2:
            odd[:, pl.ds((j // 2) * cols, cols)] = piece.astype(BF16)
        else:
            even[:, pl.ds((j // 2 - 1) * cols, cols)] = piece


def final_kernel(*refs):
    out = refs[-1]
    for i in range(2):
        own, near, far = refs[3 * i : 3 * i + 3]
        rows, cols = own.shape
        out[pl.ds(i * rows, rows), :] = (
            own[...] + near[:, :cols].astype(F32) + far[...].astype(F32)
        ).astype(BF16)


def flip(array, axis, bit):
    size = lax.axis_size(axis)
    return lax.ppermute(array, axis, [(i, i ^ bit) for i in range(size)])


def gather_flips(array, axis):
    size = lax.axis_size(axis)
    parts = {0: array}
    bit = size // 2
    while bit:
        for k in list(parts):
            parts[k ^ bit] = flip(parts[k], axis, bit)
        bit //= 2
    return [parts[k] for k in range(size)]


def grant(mebibytes):
    return pltpu.CompilerParams(vmem_limit_bytes=mebibytes << 20)


def shaped(shape, dtype):
    return jax.ShapeDtypeStruct(shape, dtype)


def in_hbm(array):
    return pltpu.with_memory_space_constraint(array, pltpu.HBM)


def exchange(array):
    return lax.all_to_all(array, "seq", split_axis=0, concat_axis=0, tiled=True)


def on_device(
    child_feat,
    parent_feat,
    child_parent,
    owner,
    log_gate,
    norm_gain,
    w_query,
    w_key,
    w_value,
    head_gain,
    w_out,
    ffn_gain,
    w_up,
    w_down,
):
    blocks = lax.axis_size("seq")
    groups = lax.axis_size("ffn")
    heads, slots = log_gate.shape
    cap = slots // blocks
    tokens, width = child_feat.shape
    share = w_query.shape[1]
    hd = share // heads
    cols = width // groups

    child_feat, parent_feat, w_query, w_key, w_value, w_up, w_down = map(
        in_hbm, (child_feat, parent_feat, w_query, w_key, w_value, w_up, w_down)
    )
    arrived = exchange(log_gate.reshape(heads, blocks, cap).transpose(1, 0, 2))
    if cap % LANES:
        arrived = arrived.transpose(1, 0, 2).reshape(heads, slots)
    wout_parts = [in_hbm(part) for part in gather_flips(w_out, "ffn")]

    tiles = pl.cdiv(tokens, min(256, tokens))
    joined, q, k, v, taken, own = pl.pallas_call(
        functools.partial(pre_kernel, cap, blocks),
        out_shape=(
            pltpu.HBM((tokens, width), BF16),
            shaped((tokens, share), BF16),
            shaped((tokens, share), BF16),
            shaped((tokens, share), BF16),
            shaped((tokens, slots), BF16),
            shaped((1, tokens), jnp.int32),
        ),
        in_specs=[HBM] * 8,
        out_specs=[HBM] + [VMEM] * 5,
        scratch_shapes=[
            pltpu.VMEM((tokens, width), BF16),
            pltpu.VMEM(parent_feat.shape, BF16),
            pltpu.VMEM((1, tokens), jnp.int32),
            pltpu.VMEM((1, tokens), jnp.int32),
            pltpu.VMEM((width,), BF16),
            pltpu.VMEM((3, width, share), BF16),
            pltpu.VMEM((tokens, width), BF16),
            pltpu.SemaphoreType.DMA((7 + tiles,)),
            pltpu.SemaphoreType.DMA((tiles,)),
        ],
        name="pre",
        compiler_params=grant(20),
    )(
        child_feat,
        parent_feat,
        in_hbm(child_parent.reshape(1, tokens)),
        in_hbm(owner.reshape(1, tokens)),
        in_hbm(norm_gain),
        w_query,
        w_key,
        w_value,
    )

    half = blocks // 2
    seats = 8 * pl.cdiv(half, 8)
    sent = shaped((half * hd + 2 * seats, share), BF16)
    held = shaped((half, hd, share), F32)
    rate = shaped((seats, share), F32)
    c_lanes, c_rows, *made = pl.pallas_call(
        functools.partial(state_kernel, cap, blocks, hd),
        out_shape=(shaped((tokens, share), F32), shaped((8, tokens), F32)) + (sent, held, rate) * 2,
        in_specs=[VMEM] * 5,
        out_specs=[VMEM] * 8,
        name="state",
        compiler_params=grant(12 if blocks <= 8 else 24),
    )(taken, arrived, k, v, own)
    scans = [made[:3], made[3:]]

    inside = pl.pallas_call(
        functools.partial(inside_kernel, hd),
        out_shape=shaped((tokens, share), F32),
        in_specs=[VMEM] * 6,
        out_specs=VMEM,
        name="inside",
        compiler_params=grant(12),
    )(q, k, v, c_lanes, c_rows, own)

    bits = [1 << i for i in range(blocks.bit_length() - 1)]
    for bit in bits:
        for g in range(2):
            came = flip(scans[g][0], "seq", bit)
            if bit == bits[-1]:
                scans[g] = [came, *scans[g][1:]]
                continue
            scans[g] = pl.pallas_call(
                functools.partial(step_kernel, bit, hd, bit == 1),
                out_shape=(sent, held, rate, held, rate),
                in_specs=[VMEM] * len(scans[g]),
                out_specs=[VMEM] * 5,
                compiler_params=grant(6 if blocks <= 8 else 24),
            )(came, *scans[g][1:])

    flats = pl.pallas_call(
        functools.partial(outside_kernel, bits[-1], hd),
        out_shape=(shaped((tokens // 2, share), BF16),) * 2,
        in_specs=[VMEM] * 15,
        out_specs=[VMEM] * 2,
        scratch_shapes=[
            pltpu.VMEM((tokens, blocks * share), BF16),
            pltpu.VMEM((blocks * share, share), BF16),
        ],
        name="outside",
        compiler_params=grant(12 if blocks <= 8 else 52),
    )(*scans[0], *scans[1], q, own, c_lanes, inside, head_gain.reshape(1, share))

    rows, half = tokens // 2, groups // 2
    parts = [gather_flips(flat, "ffn") for flat in flats]
    load = pl.pallas_call(
        functools.partial(load_kernel, groups),
        out_shape=(
            pltpu.VMEM((tokens, width), F32),
            pltpu.VMEM((groups - 2, share, width), BF16),
            pltpu.VMEM((1, width), F32),
            pltpu.VMEM(w_up.shape, BF16),
            pltpu.VMEM(w_down.shape, BF16),
        ),
        in_specs=[VMEM] * 4 + [HBM] * (groups + 4),
        out_specs=[VMEM] * 5,
        scratch_shapes=[
            pltpu.VMEM((tokens, width), BF16),
            pltpu.VMEM((width,), BF16),
            pltpu.VMEM((2, share, width), BF16),
            pltpu.SemaphoreType.DMA((groups + 4,)),
        ],
        name="load",
        compiler_params=grant(12),
    )
    loaded = load(
        parts[0][0],
        parts[1][0],
        parts[0][1],
        parts[1][1],
        *wout_parts,
        in_hbm(joined),
        in_hbm(ffn_gain),
        w_up,
        w_down,
    )
    finals = []
    for i in range(2):
        kept, even, odd = pl.pallas_call(
            functools.partial(ffn_kernel, groups, i * rows),
            out_shape=(
                shaped((rows, cols), F32),
                shaped((rows, max(half - 1, 1) * cols), F32),
                shaped((rows, half * cols), BF16),
            ),
            in_specs=[VMEM] * (groups + 3),
            out_specs=[VMEM] * 3,
            scratch_shapes=[pltpu.VMEM((rows, width), F32)],
            compiler_params=grant(12),
        )(*parts[i][2:], *loaded)
        near = flip(odd, "ffn", 1)
        pieces = {
            j: (
                even[:, (j // 2 - 1) * cols : j // 2 * cols]
                + near[:, j // 2 * cols : (j // 2 + 1) * cols].astype(F32)
            )
            for j in range(2, groups, 2)
        }
        far = [flip(pieces[j].astype(BF16), "ffn", j) for j in pieces]
        far = far[0] if len(far) == 1 else sum(part.astype(F32) for part in far)
        finals += [kept, near, far]
    return pl.pallas_call(
        final_kernel,
        out_shape=shaped((tokens, cols), BF16),
        in_specs=[VMEM] * 6,
        out_specs=VMEM,
        name="final",
        compiler_params=grant(8),
    )(*finals)


def solution(mesh):
    in_specs = (
        P("seq", None),
        P("seq", None),
        P("seq"),
        P("seq", None),
        P("ffn", "seq"),
        P(),
        P(None, "ffn"),
        P(None, "ffn"),
        P(None, "ffn"),
        P("ffn"),
        P("ffn", None),
        P(),
        P(None, "ffn"),
        P("ffn", None),
    )

    return jax.shard_map(
        on_device, mesh=mesh, in_specs=in_specs, out_specs=P("seq", "ffn"), check_vma=False
    )
```

```python
import functools

import jax
import jax.numpy as jnp
from jax import lax
from jax.experimental import pallas as pl
from jax.experimental.pallas import tpu as pltpu
from jax.sharding import PartitionSpec as P


EPSILON = 1e-05
F32 = jnp.float32
BF16 = jnp.bfloat16
LANES = 128
SPLIT = 12
NT = (((1,), (1,)), ((), ()))
TN = (((0,), (0,)), ((), ()))
VMEM = pl.BlockSpec(memory_space=pltpu.VMEM)
HBM = pl.BlockSpec(memory_space=pltpu.HBM)


def split3(values):
    high = values.astype(BF16)
    rest = values - high.astype(F32)
    middle = rest.astype(BF16)
    low = (rest - middle.astype(F32)).astype(BF16)
    return high, middle, low


def dot(a, b):
    return jnp.dot(a, b, preferred_element_type=F32)


def iota(shape, dim):
    return lax.broadcasted_iota(jnp.int32, shape, dim)


def row_norm(values, scales):
    return values * lax.rsqrt(jnp.mean(values * values, axis=-1, keepdims=True) + EPSILON) * scales


def column(row, width=LANES):
    return jnp.broadcast_to(row, (width, row.shape[1])).T


def head_of_lane(shape, hd):
    return iota(shape, len(shape) - 1) // hd


def fetch(pairs, sems):
    copies = [pltpu.make_async_copy(src, dst, sems.at[i]) for i, (src, dst) in enumerate(pairs)]
    for copy in copies:
        copy.start()
    return copies


def pre_kernel(
    cap, blocks, cf, pf, pick, own, gain, wq, wk, wv,
    joined, q, k, v, taken, own_out,
    cf_v, pf_v, pick_v, own_v, gain_v, w_v, joined_v, sems, out_sems,
):
    tokens = cf.shape[0]
    parents = pf.shape[0]
    tile = min(256, tokens)
    starts = range(0, tokens, tile)
    small = fetch(
        [(own, own_v), (pick, pick_v), (pf, pf_v), (gain, gain_v)]
        + [(cf.at[pl.ds(at, tile)], cf_v.at[pl.ds(at, tile)]) for at in starts]
        + [(w, w_v.at[i]) for i, w in enumerate((wq, wk, wv))],
        sems,
    )
    parts, weights = small[4 : 4 + len(starts)], small[4 + len(starts) :]
    small[0].wait()
    owners = own_v[...]
    own_out[...] = owners
    lane = iota((1, blocks * cap), 1)
    lane_owner, lane_rank = lane // cap, lane % cap
    ones = jnp.ones((tokens, LANES), BF16)
    for at in starts:
        rows = pl.ds(at, tile)
        mine = column(own_v[:, rows])
        same = (mine[:, :1] == owners) & (iota((tile, tokens), 0) + at >= iota((tile, tokens), 1))
        count = dot(jnp.where(same, 1.0, 0.0).astype(BF16), ones)
        rank = count[:, :1].astype(jnp.int32) - 1
        kept = (mine[:, :1] == lane_owner) & (lane_rank <= rank)
        taken[rows, :] = jnp.where(kept, 1.0, 0.0).astype(BF16)
    for copy in small[1:4]:
        copy.wait()
    scales = gain_v[...].astype(F32).reshape(1, -1)
    stores = []
    for i, at in enumerate(starts):
        rows = pl.ds(at, tile)
        parts[i].wait()
        chosen = jnp.where(iota((parents, tile), 0) == pick_v[:, rows], 1.0, 0.0).astype(BF16)
        added = lax.dot_general(chosen, pf_v[...], TN, preferred_element_type=F32)
        summed = (cf_v[rows, :].astype(F32) + added).astype(BF16)
        joined_v[rows, :] = summed
        store = pltpu.make_async_copy(joined_v.at[rows], joined.at[rows], out_sems.at[i])
        store.start()
        stores.append(store)
        normed = row_norm(summed.astype(F32), scales).astype(BF16)
        if i == 0:
            for copy in weights:
                copy.wait()
        for j, out in enumerate((q, k, v)):
            out[rows, :] = dot(normed, w_v[j]).astype(BF16)
    for store in stores:
        store.wait()


def gate_rows(gates, blocks):
    if len(gates.shape) == 3:
        rows = jnp.concatenate([gates[o] for o in range(blocks)], axis=1)
    else:
        rows = gates[...]
    heads = rows.shape[0]
    rows = jnp.concatenate([rows, jnp.zeros((8 - heads, rows.shape[1]), F32)], axis=0)
    return jnp.concatenate([part.astype(F32) for part in split3(rows)], axis=0).astype(BF16)


def seat(owner, blocks):
    half = max(blocks // 2, 1)
    return owner // half * (8 * pl.cdiv(half, 8)) + owner % half


def put_tail(send, decay, at):
    high = decay.astype(BF16)
    low = decay - high.astype(F32)
    send[at:, :] = jnp.concatenate([high.astype(F32), low], axis=0).astype(BF16)


def state_kernel(cap, blocks, hd, taken, gates, k, v, own, c_lanes, c_rows, *outs):
    tokens, share = k.shape
    half = blocks // 2
    rows = 8 * pl.cdiv(half, 8)
    table = gate_rows(gates, blocks)
    slots = table.shape[1]
    summed = lax.dot_general(taken[...], table, NT, preferred_element_type=F32)
    lanes = LANES * pl.cdiv(2 * rows, LANES)
    chunk = jnp.where(
        seat(iota((slots, lanes), 0) // cap, blocks) == iota((slots, lanes), 1), 1.0, 0.0
    ).astype(BF16)
    totals = dot(table, chunk)
    totals = jnp.concatenate(
        [part.astype(F32) for part in split3(totals[:8] + totals[8:16] + totals[16:])], axis=0
    ).astype(BF16)
    mine = column(seat(own[...], blocks))[:, :1]
    named = jnp.where(mine == iota((tokens, lanes), 1), 1.0, 0.0).astype(BF16)
    whole = lax.dot_general(named, totals, NT, preferred_element_type=F32)
    summed = jnp.concatenate([summed, whole], axis=0)
    spread = jnp.where(
        iota((24, share), 0) % 8 == head_of_lane((24, share), hd), 1.0, 0.0
    ).astype(BF16)
    wide = sum(dot(part, spread) for part in split3(summed))
    c_lanes[...] = wide[:tokens]
    turned_c = lax.dot_general(table, taken[...], NT, preferred_element_type=F32)
    c_rows[...] = turned_c[:8] + turned_c[8:16] + turned_c[16:]
    faded = k[...].astype(F32) * jnp.exp(jnp.minimum(wide[tokens:] - wide[:tokens], 0.0))
    turned = faded.astype(BF16).T
    decays = jnp.exp(lax.dot_general(totals, spread, TN, preferred_element_type=F32))
    owners = own[...]
    values = v[...]
    lane_head = head_of_lane((hd, share), hd)
    for g in range(2):
        send, state, decay = outs[3 * g : 3 * g + 3]

        def one(i, nothing):
            masked = jnp.where(owners == i + g * half, turned, jnp.zeros_like(turned))
            full = dot(masked, values)
            packed = jnp.zeros((hd, share), F32)
            for h in range(share // hd):
                packed = jnp.where(lane_head == h, full[h * hd : (h + 1) * hd], packed)
            state[i] = packed
            send[pl.ds(pl.multiple_of(i * hd, hd), hd), :] = packed.astype(BF16)
            return nothing

        lax.fori_loop(0, half, one, 0, unroll=blocks <= 8)
        decay[...] = decays[g * rows : (g + 1) * rows]
        put_tail(send, decay[...], half * hd)


def joined_scan(bit, hd, refs):
    came, state, decay, prefix, lead = refs
    half = state.shape[0]
    rows = decay.shape[0]
    upper = ((lax.axis_index("seq") & bit) // bit).astype(F32)
    tail = came[half * hd :, :].astype(F32)
    theirs_decay = tail[:rows] + tail[rows:]
    mine_decay = decay[...]
    past = jnp.ones_like(mine_decay) if lead is None else lead[...]
    scale_mine = upper + (1.0 - upper) * theirs_decay
    scale_theirs = upper * mine_decay + (1.0 - upper)
    add = upper * past
    pairs = []
    for i in range(half):
        theirs = came[i * hd : (i + 1) * hd, :].astype(F32)
        total = scale_mine[i : i + 1] * state[i] + scale_theirs[i : i + 1] * theirs
        before = add[i : i + 1] * theirs
        pairs.append((total, before if prefix is None else prefix[i] + before))
    return pairs, mine_decay * theirs_decay, past * scale_mine_lead(upper, theirs_decay)


def scale_mine_lead(upper, theirs_decay):
    return upper * theirs_decay + (1.0 - upper)


def step_kernel(bit, hd, first, *refs):
    came, state, decay = refs[:3]
    prefix, lead = (None, None) if first else refs[3:5]
    send, state_out, decay_out, prefix_out, lead_out = refs[-5:]
    pairs, total_decay, total_lead = joined_scan(bit, hd, (came, state, decay, prefix, lead))
    for i, (total, before) in enumerate(pairs):
        state_out[i] = total
        prefix_out[i] = before
        send[i * hd : (i + 1) * hd, :] = total.astype(BF16)
    decay_out[...] = total_decay
    lead_out[...] = total_lead
    put_tail(send, total_decay, len(pairs) * hd)


def inside_kernel(hd, q, k, v, c_lanes, c_rows, own, inside):
    tokens, share = q.shape
    heads = share // hd
    tile = min(256, tokens)
    for at in range(0, tokens, tile):
        rows = pl.ds(at, tile)
        reach = at + tile
        mine = column(own[:, rows])[:, :1]
        same = (mine == own[:, :reach]) & (
            iota((tile, reach), 0) + at >= iota((tile, reach), 1)
        )
        queries = q[rows, :]
        keys = k[:reach, :]
        values = v[:reach, :]
        total = jnp.zeros((tile, share), F32)
        for h in range(heads):
            only = head_of_lane((tile, share), hd) == h
            scores = lax.dot_general(
                jnp.where(only, queries, jnp.zeros_like(queries)),
                keys,
                NT,
                preferred_element_type=F32,
            )
            gap = c_lanes[rows, h * hd : h * hd + 1] - c_rows[h : h + 1, :reach]
            decay = jnp.where(same, jnp.exp(jnp.where(same, gap, 0.0)), 0.0)
            mixing = (scores * decay).astype(BF16)
            only = head_of_lane((reach, share), hd) == h
            total += dot(mixing, jnp.where(only, values, jnp.zeros_like(values)))
        inside[rows, :] = total


def outside_kernel(bit, owners, hd, *refs):
    pairs, whole, lead = joined_scan(bit, hd, refs[:5])
    q, own, *refs = refs[5:]
    carry = jnp.zeros(pairs[0][0].shape, F32) if owners[0] == 0 else refs.pop(0)[...]
    _, share = q.shape
    heads = share // hd
    mine = column(own[...])[:, :1]
    queries = q[...]
    block_diagonal = iota((share, share), 0) // hd == iota((share, share), 1) // hd
    wide, table = refs[-2:]
    for i, (total, before) in enumerate(pairs):
        state = before + lead[i : i + 1] * carry
        stacked = jnp.concatenate([state] * heads, axis=0)
        at = pl.ds(i * share, share)
        table[at, :] = jnp.where(block_diagonal, stacked, 0.0).astype(BF16)
        wide[:, at] = jnp.where(mine == owners[i], queries, jnp.zeros_like(queries))
        carry = whole[i : i + 1] * carry + total
    outside = dot(wide[...], table[...])
    if owners[0] == 0:
        part, carried = refs[:2]
        part[...] = outside
        carried[...] = carry
        return
    earlier, c_lanes, inside, gain, both, first, second = refs[:7]
    combined = inside[...] + (outside + earlier[...]) * jnp.exp(c_lanes[...])
    square = combined * combined
    mean = jnp.where(block_diagonal, 1.0 / hd, 0.0).astype(BF16)
    spread = sum(dot(part, mean) for part in split3(square))
    flat = (combined * lax.rsqrt(spread + EPSILON) * gain[...].astype(F32)).astype(BF16)
    both[...] = flat
    first[...] = flat[: first.shape[0]]
    second[...] = flat[first.shape[0] :]


def fetch_kernel(*refs):
    sources, gain, outs, (scale, gain_v, sems) = refs[:4], refs[4], refs[5:9], refs[9:]
    copies = fetch([(gain, gain_v), *zip(sources, outs)], sems)
    copies[0].wait()
    scale[...] = gain_v[...].astype(F32).reshape(1, -1)
    for copy in copies[1:]:
        copy.wait()


def own_kernel(mine, near, own_w, near_w, joined, hidden):
    tokens = joined.shape[0]
    tile = min(256, tokens)
    for at in range(0, tokens, tile):
        rows = pl.ds(at, tile)
        hidden[rows, :] = (
            joined[rows, :].astype(F32)
            + dot(mine[rows, :], own_w[...])
            + dot(near[rows, :], near_w[...])
        )


def ffn_kernel(groups, at, *refs):
    flats, wouts = refs[: groups - 2], refs[groups - 2 : 2 * (groups - 2)]
    hidden_v, scale, up_v, down_v, own, even, odd, scratch = refs[2 * (groups - 2) :]
    mine = lax.axis_index("ffn")
    rows, cols = own.shape
    hidden = hidden_v[pl.ds(at, rows), :]
    for flat, wout in zip(flats, wouts):
        hidden = hidden + dot(flat[...], wout[...])
    scratch[...] = hidden
    second = row_norm(hidden, scale[...]).astype(BF16)
    expanded = jax.nn.gelu(dot(second, up_v[...])).astype(BF16)
    for j in sorted(range(groups), key=lambda j: -(j % 2)):
        target = pl.ds(pl.multiple_of((mine ^ j) * cols, cols), cols)
        piece = dot(expanded, down_v[:, target])
        if j == 0:
            own[...] = piece + scratch[:, target]
        elif j % 2:
            odd[:, pl.ds((j // 2) * cols, cols)] = piece.astype(BF16)
        else:
            even[:, pl.ds((j // 2 - 1) * cols, cols)] = piece


def final_kernel(*refs):
    out = refs[-1]
    at = 0
    for i in range(2):
        own, near, far = refs[3 * i : 3 * i + 3]
        rows, cols = own.shape
        place = pl.ds(at, rows)
        at += rows
        out[place, :] = (
            own[...] + near[:, :cols].astype(F32) + far[...].astype(F32)
        ).astype(BF16)


def flip(array, axis, bit):
    size = lax.axis_size(axis)
    return lax.ppermute(array, axis, [(i, i ^ bit) for i in range(size)])


def gather_flips(array, axis):
    size = lax.axis_size(axis)
    parts = {0: array}
    bit = size // 2
    while bit:
        for k in list(parts):
            parts[k ^ bit] = flip(parts[k], axis, bit)
        bit //= 2
    return [parts[k] for k in range(size)]


def grant(mebibytes):
    return pltpu.CompilerParams(vmem_limit_bytes=mebibytes << 20)


def shaped(shape, dtype):
    return jax.ShapeDtypeStruct(shape, dtype)


def in_hbm(array):
    return pltpu.with_memory_space_constraint(array, pltpu.HBM)


def exchange(array):
    return lax.all_to_all(array, "seq", split_axis=0, concat_axis=0, tiled=True)


def on_device(
    child_feat,
    parent_feat,
    child_parent,
    owner,
    log_gate,
    norm_gain,
    w_query,
    w_key,
    w_value,
    head_gain,
    w_out,
    ffn_gain,
    w_up,
    w_down,
):
    blocks = lax.axis_size("seq")
    groups = lax.axis_size("ffn")
    heads, slots = log_gate.shape
    cap = slots // blocks
    tokens, width = child_feat.shape
    share = w_query.shape[1]
    hd = share // heads
    cols = width // groups

    child_feat, parent_feat, w_query, w_key, w_value, w_up, w_down = map(
        in_hbm, (child_feat, parent_feat, w_query, w_key, w_value, w_up, w_down)
    )
    arrived = exchange(log_gate.reshape(heads, blocks, cap).transpose(1, 0, 2))
    if cap % LANES:
        arrived = arrived.transpose(1, 0, 2).reshape(heads, slots)
    wout_parts = gather_flips(w_out, "ffn")

    tiles = pl.cdiv(tokens, min(256, tokens))
    joined, q, k, v, taken, own = pl.pallas_call(
        functools.partial(pre_kernel, cap, blocks),
        out_shape=(
            pltpu.HBM((tokens, width), BF16),
            shaped((tokens, share), BF16),
            shaped((tokens, share), BF16),
            shaped((tokens, share), BF16),
            shaped((tokens, slots), BF16),
            shaped((1, tokens), jnp.int32),
        ),
        in_specs=[HBM] * 8,
        out_specs=[HBM] + [VMEM] * 5,
        scratch_shapes=[
            pltpu.VMEM((tokens, width), BF16),
            pltpu.VMEM(parent_feat.shape, BF16),
            pltpu.VMEM((1, tokens), jnp.int32),
            pltpu.VMEM((1, tokens), jnp.int32),
            pltpu.VMEM((width,), BF16),
            pltpu.VMEM((3, width, share), BF16),
            pltpu.VMEM((tokens, width), BF16),
            pltpu.SemaphoreType.DMA((7 + tiles,)),
            pltpu.SemaphoreType.DMA((tiles,)),
        ],
        name="pre",
        compiler_params=grant(20),
    )(
        child_feat,
        parent_feat,
        in_hbm(child_parent.reshape(1, tokens)),
        in_hbm(owner.reshape(1, tokens)),
        in_hbm(norm_gain),
        w_query,
        w_key,
        w_value,
    )

    half = blocks // 2
    seats = 8 * pl.cdiv(half, 8)
    sent = shaped((half * hd + 2 * seats, share), BF16)
    held = shaped((half, hd, share), F32)
    rate = shaped((seats, share), F32)
    c_lanes, c_rows, *made = pl.pallas_call(
        functools.partial(state_kernel, cap, blocks, hd),
        out_shape=(shaped((tokens, share), F32), shaped((8, tokens), F32)) + (sent, held, rate) * 2,
        in_specs=[VMEM] * 5,
        out_specs=[VMEM] * 8,
        name="state",
        compiler_params=grant(12 if blocks <= 8 else 24),
    )(taken, arrived, k, v, own)
    scans = [made[:3], made[3:]]

    inside = pl.pallas_call(
        functools.partial(inside_kernel, hd),
        out_shape=shaped((tokens, share), F32),
        in_specs=[VMEM] * 6,
        out_specs=VMEM,
        name="inside",
        compiler_params=grant(12),
    )(q, k, v, c_lanes, c_rows, own)

    bits = [1 << i for i in range(blocks.bit_length() - 1)]
    for bit in bits:
        for g in range(2):
            came = flip(scans[g][0], "seq", bit)
            if bit == bits[-1]:
                scans[g] = [came, *scans[g][1:]]
                continue
            scans[g] = pl.pallas_call(
                functools.partial(step_kernel, bit, hd, bit == 1),
                out_shape=(sent, held, rate, held, rate),
                in_specs=[VMEM] * len(scans[g]),
                out_specs=[VMEM] * 5,
                compiler_params=grant(6 if blocks <= 8 else 24),
            )(came, *scans[g][1:])

    split = tokens * SPLIT // 16
    sizes = (split, tokens - split)
    scratch = [
        pltpu.VMEM((tokens, half * share), BF16),
        pltpu.VMEM((half * share, share), BF16),
    ]
    earlier, carried = pl.pallas_call(
        functools.partial(outside_kernel, bits[-1], range(half), hd),
        out_shape=(shaped((tokens, share), F32), shaped((hd, share), F32)),
        in_specs=[VMEM] * 7,
        out_specs=[VMEM] * 2,
        scratch_shapes=scratch,
        name="outside0",
        compiler_params=grant(8 if blocks <= 8 else 40),
    )(*scans[0], q, own)
    flat, *flats = pl.pallas_call(
        functools.partial(outside_kernel, bits[-1], range(half, blocks), hd),
        out_shape=tuple(shaped((rows, share), BF16) for rows in (tokens,) + sizes),
        in_specs=[VMEM] * 12,
        out_specs=[VMEM] * 3,
        scratch_shapes=scratch,
        name="outside1",
        compiler_params=grant(8 if blocks <= 8 else 40),
    )(*scans[1], q, own, carried, earlier, c_lanes, inside, head_gain.reshape(1, share))

    fetched = pl.pallas_call(
        fetch_kernel,
        out_shape=(
            pltpu.VMEM((tokens, width), BF16),
            pltpu.VMEM(w_out.shape, BF16),
            pltpu.VMEM(w_up.shape, BF16),
            pltpu.VMEM(w_down.shape, BF16),
            pltpu.VMEM((1, width), F32),
        ),
        in_specs=[HBM] * 5,
        out_specs=[VMEM] * 5,
        scratch_shapes=[pltpu.VMEM((width,), BF16), pltpu.SemaphoreType.DMA((5,))],
        name="fetch",
        compiler_params=grant(2),
    )(in_hbm(joined), in_hbm(w_out), w_up, w_down, in_hbm(ffn_gain))

    near_flat = flip(flat, "ffn", 1)
    parts = [gather_flips(part, "ffn") for part in flats]
    hidden = pl.pallas_call(
        own_kernel,
        out_shape=pltpu.VMEM((tokens, width), F32),
        in_specs=[VMEM] * 5,
        out_specs=VMEM,
        name="own",
        compiler_params=grant(6),
    )(flat, near_flat, fetched[1], wout_parts[1], fetched[0])
    finals = []
    for i, rows in enumerate(sizes):
        kept, even, odd = pl.pallas_call(
            functools.partial(ffn_kernel, groups, i * split),
            out_shape=(
                shaped((rows, cols), F32),
                shaped((rows, max(groups // 2 - 1, 1) * cols), F32),
                shaped((rows, groups // 2 * cols), BF16),
            ),
            in_specs=[VMEM] * (2 * groups),
            out_specs=[VMEM] * 3,
            scratch_shapes=[pltpu.VMEM((rows, width), F32)],
            compiler_params=grant(10),
        )(*parts[i][2:], *wout_parts[2:], hidden, fetched[4], *fetched[2:4])
        near = flip(odd, "ffn", 1)
        pieces = {
            j: (
                even[:, (j // 2 - 1) * cols : j // 2 * cols]
                + near[:, j // 2 * cols : (j // 2 + 1) * cols].astype(F32)
            )
            for j in range(2, groups, 2)
        }
        far = [flip(pieces[j].astype(BF16), "ffn", j) for j in pieces]
        far = far[0] if len(far) == 1 else sum(part.astype(F32) for part in far)
        finals += [kept, near, far]
    return pl.pallas_call(
        final_kernel,
        out_shape=shaped((tokens, cols), BF16),
        in_specs=[VMEM] * 6,
        out_specs=VMEM,
        name="final",
        compiler_params=grant(8),
    )(*finals)


def solution(mesh):
    in_specs = (
        P("seq", None),
        P("seq", None),
        P("seq"),
        P("seq", None),
        P("ffn", "seq"),
        P(),
        P(None, "ffn"),
        P(None, "ffn"),
        P(None, "ffn"),
        P("ffn"),
        P("ffn", None),
        P(),
        P(None, "ffn"),
        P("ffn", None),
    )

    return jax.shard_map(
        on_device, mesh=mesh, in_specs=in_specs, out_specs=P("seq", "ffn"), check_vma=False
    )
```

```python
import functools

import jax
import jax.numpy as jnp
from jax import lax
from jax.experimental import pallas as pl
from jax.experimental.pallas import tpu as pltpu
from jax.sharding import PartitionSpec as P


EPSILON = 1e-05
F32 = jnp.float32
BF16 = jnp.bfloat16
LANES = 128
SPLIT = 12
NT = (((1,), (1,)), ((), ()))
TN = (((0,), (0,)), ((), ()))
VMEM = pl.BlockSpec(memory_space=pltpu.VMEM)
HBM = pl.BlockSpec(memory_space=pltpu.HBM)


def split3(values):
    high = values.astype(BF16)
    rest = values - high.astype(F32)
    middle = rest.astype(BF16)
    low = (rest - middle.astype(F32)).astype(BF16)
    return high, middle, low


def dot(a, b):
    return jnp.dot(a, b, preferred_element_type=F32)


def iota(shape, dim):
    return lax.broadcasted_iota(jnp.int32, shape, dim)


def row_norm(values, scales):
    return values * lax.rsqrt(jnp.mean(values * values, axis=-1, keepdims=True) + EPSILON) * scales


def column(row, width=LANES):
    return jnp.broadcast_to(row, (width, row.shape[1])).T


def head_of_lane(shape, hd):
    return iota(shape, len(shape) - 1) // hd


def fetch(pairs, sems):
    copies = [pltpu.make_async_copy(src, dst, sems.at[i]) for i, (src, dst) in enumerate(pairs)]
    for copy in copies:
        copy.start()
    return copies


def pre_kernel(
    cap, blocks, cf, pf, pick, own, gain, wq, wk, wv,
    joined, q, k, v, taken, own_out,
    cf_v, pf_v, pick_v, own_v, gain_v, w_v, sems,
):
    tokens = cf.shape[0]
    parents = pf.shape[0]
    tile = min(256, tokens)
    starts = range(0, tokens, tile)
    small = fetch(
        [(own, own_v), (pick, pick_v), (pf, pf_v), (gain, gain_v)]
        + [(cf.at[pl.ds(at, tile)], cf_v.at[pl.ds(at, tile)]) for at in starts]
        + [(w, w_v.at[i]) for i, w in enumerate((wq, wk, wv))],
        sems,
    )
    parts, weights = small[4 : 4 + len(starts)], small[4 + len(starts) :]
    small[0].wait()
    owners = own_v[...]
    own_out[...] = owners
    lane = iota((1, blocks * cap), 1)
    lane_owner, lane_rank = lane // cap, lane % cap
    ones = jnp.ones((tokens, LANES), BF16)
    for at in starts:
        rows = pl.ds(at, tile)
        mine = column(own_v[:, rows])
        same = (mine[:, :1] == owners) & (iota((tile, tokens), 0) + at >= iota((tile, tokens), 1))
        count = dot(jnp.where(same, 1.0, 0.0).astype(BF16), ones)
        rank = count[:, :1].astype(jnp.int32) - 1
        kept = (mine[:, :1] == lane_owner) & (lane_rank <= rank)
        taken[rows, :] = jnp.where(kept, 1.0, 0.0).astype(BF16)
    for copy in small[1:4]:
        copy.wait()
    scales = gain_v[...].astype(F32).reshape(1, -1)
    for i, at in enumerate(starts):
        rows = pl.ds(at, tile)
        parts[i].wait()
        chosen = jnp.where(iota((parents, tile), 0) == pick_v[:, rows], 1.0, 0.0).astype(BF16)
        added = lax.dot_general(chosen, pf_v[...], TN, preferred_element_type=F32)
        summed = (cf_v[rows, :].astype(F32) + added).astype(BF16)
        joined[rows, :] = summed
        normed = row_norm(summed.astype(F32), scales).astype(BF16)
        if i == 0:
            for copy in weights:
                copy.wait()
        for j, out in enumerate((q, k, v)):
            out[rows, :] = dot(normed, w_v[j]).astype(BF16)


def gate_rows(gates, blocks):
    if len(gates.shape) == 3:
        rows = jnp.concatenate([gates[o] for o in range(blocks)], axis=1)
    else:
        rows = gates[...]
    heads = rows.shape[0]
    rows = jnp.concatenate([rows, jnp.zeros((8 - heads, rows.shape[1]), F32)], axis=0)
    return jnp.concatenate([part.astype(F32) for part in split3(rows)], axis=0).astype(BF16)


def seat(owner, blocks):
    half = max(blocks // 2, 1)
    return owner // half * (8 * pl.cdiv(half, 8)) + owner % half


def put_tail(send, decay, at):
    high = decay.astype(BF16)
    low = decay - high.astype(F32)
    send[at:, :] = jnp.concatenate([high.astype(F32), low], axis=0).astype(BF16)


def state_kernel(cap, blocks, hd, taken, gates, k, v, own, c_lanes, c_rows, *outs):
    tokens, share = k.shape
    half = blocks // 2
    rows = 8 * pl.cdiv(half, 8)
    table = gate_rows(gates, blocks)
    slots = table.shape[1]
    summed = lax.dot_general(taken[...], table, NT, preferred_element_type=F32)
    lanes = LANES * pl.cdiv(2 * rows, LANES)
    chunk = jnp.where(
        seat(iota((slots, lanes), 0) // cap, blocks) == iota((slots, lanes), 1), 1.0, 0.0
    ).astype(BF16)
    totals = dot(table, chunk)
    totals = jnp.concatenate(
        [part.astype(F32) for part in split3(totals[:8] + totals[8:16] + totals[16:])], axis=0
    ).astype(BF16)
    mine = column(seat(own[...], blocks))[:, :1]
    named = jnp.where(mine == iota((tokens, lanes), 1), 1.0, 0.0).astype(BF16)
    whole = lax.dot_general(named, totals, NT, preferred_element_type=F32)
    summed = jnp.concatenate([summed, whole], axis=0)
    spread = jnp.where(
        iota((24, share), 0) % 8 == head_of_lane((24, share), hd), 1.0, 0.0
    ).astype(BF16)
    wide = sum(dot(part, spread) for part in split3(summed))
    c_lanes[...] = wide[:tokens]
    turned_c = lax.dot_general(table, taken[...], NT, preferred_element_type=F32)
    c_rows[...] = turned_c[:8] + turned_c[8:16] + turned_c[16:]
    faded = k[...].astype(F32) * jnp.exp(jnp.minimum(wide[tokens:] - wide[:tokens], 0.0))
    turned = faded.astype(BF16).T
    decays = jnp.exp(lax.dot_general(totals, spread, TN, preferred_element_type=F32))
    owners = own[...]
    values = v[...]
    lane_head = head_of_lane((hd, share), hd)
    for g in range(2):
        send, state, decay = outs[3 * g : 3 * g + 3]

        def one(i, nothing):
            masked = jnp.where(owners == i + g * half, turned, jnp.zeros_like(turned))
            full = dot(masked, values)
            packed = jnp.zeros((hd, share), F32)
            for h in range(share // hd):
                packed = jnp.where(lane_head == h, full[h * hd : (h + 1) * hd], packed)
            state[i] = packed
            send[pl.ds(pl.multiple_of(i * hd, hd), hd), :] = packed.astype(BF16)
            return nothing

        lax.fori_loop(0, half, one, 0, unroll=blocks <= 8)
        decay[...] = decays[g * rows : (g + 1) * rows]
        put_tail(send, decay[...], half * hd)


def joined_scan(bit, hd, refs):
    came, state, decay, prefix, lead = refs
    half = state.shape[0]
    rows = decay.shape[0]
    upper = ((lax.axis_index("seq") & bit) // bit).astype(F32)
    tail = came[half * hd :, :].astype(F32)
    theirs_decay = tail[:rows] + tail[rows:]
    mine_decay = decay[...]
    past = jnp.ones_like(mine_decay) if lead is None else lead[...]
    scale_mine = upper + (1.0 - upper) * theirs_decay
    scale_theirs = upper * mine_decay + (1.0 - upper)
    add = upper * past
    pairs = []
    for i in range(half):
        theirs = came[i * hd : (i + 1) * hd, :].astype(F32)
        total = scale_mine[i : i + 1] * state[i] + scale_theirs[i : i + 1] * theirs
        before = add[i : i + 1] * theirs
        pairs.append((total, before if prefix is None else prefix[i] + before))
    return pairs, mine_decay * theirs_decay, past * scale_mine_lead(upper, theirs_decay)


def scale_mine_lead(upper, theirs_decay):
    return upper * theirs_decay + (1.0 - upper)


def step_kernel(bit, hd, first, *refs):
    came, state, decay = refs[:3]
    prefix, lead = (None, None) if first else refs[3:5]
    send, state_out, decay_out, prefix_out, lead_out = refs[-5:]
    pairs, total_decay, total_lead = joined_scan(bit, hd, (came, state, decay, prefix, lead))
    for i, (total, before) in enumerate(pairs):
        state_out[i] = total
        prefix_out[i] = before
        send[i * hd : (i + 1) * hd, :] = total.astype(BF16)
    decay_out[...] = total_decay
    lead_out[...] = total_lead
    put_tail(send, total_decay, len(pairs) * hd)


def inside_kernel(hd, q, k, v, c_lanes, c_rows, own, inside):
    tokens, share = q.shape
    heads = share // hd
    tile = min(256, tokens)
    for at in range(0, tokens, tile):
        rows = pl.ds(at, tile)
        reach = at + tile
        mine = column(own[:, rows])[:, :1]
        same = (mine == own[:, :reach]) & (
            iota((tile, reach), 0) + at >= iota((tile, reach), 1)
        )
        queries = q[rows, :]
        keys = k[:reach, :]
        values = v[:reach, :]
        total = jnp.zeros((tile, share), F32)
        for h in range(heads):
            only = head_of_lane((tile, share), hd) == h
            scores = lax.dot_general(
                jnp.where(only, queries, jnp.zeros_like(queries)),
                keys,
                NT,
                preferred_element_type=F32,
            )
            gap = c_lanes[rows, h * hd : h * hd + 1] - c_rows[h : h + 1, :reach]
            decay = jnp.where(same, jnp.exp(jnp.where(same, gap, 0.0)), 0.0)
            mixing = (scores * decay).astype(BF16)
            only = head_of_lane((reach, share), hd) == h
            total += dot(mixing, jnp.where(only, values, jnp.zeros_like(values)))
        inside[rows, :] = total


def outside_kernel(bit, owners, hd, *refs):
    pairs, whole, lead = joined_scan(bit, hd, refs[:5])
    q, own, *refs = refs[5:]
    carry = jnp.zeros(pairs[0][0].shape, F32) if owners[0] == 0 else refs.pop(0)[...]
    _, share = q.shape
    heads = share // hd
    mine = column(own[...])[:, :1]
    queries = q[...]
    block_diagonal = iota((share, share), 0) // hd == iota((share, share), 1) // hd
    wide, table = refs[-2:]
    for i, (total, before) in enumerate(pairs):
        state = before + lead[i : i + 1] * carry
        stacked = jnp.concatenate([state] * heads, axis=0)
        at = pl.ds(i * share, share)
        table[at, :] = jnp.where(block_diagonal, stacked, 0.0).astype(BF16)
        wide[:, at] = jnp.where(mine == owners[i], queries, jnp.zeros_like(queries))
        carry = whole[i : i + 1] * carry + total
    outside = dot(wide[...], table[...])
    if owners[0] == 0:
        part, carried = refs[:2]
        part[...] = outside
        carried[...] = carry
        return
    earlier, c_lanes, inside, gain, both, first, second = refs[:7]
    combined = inside[...] + (outside + earlier[...]) * jnp.exp(c_lanes[...])
    square = combined * combined
    mean = jnp.where(block_diagonal, 1.0 / hd, 0.0).astype(BF16)
    spread = sum(dot(part, mean) for part in split3(square))
    flat = (combined * lax.rsqrt(spread + EPSILON) * gain[...].astype(F32)).astype(BF16)
    both[...] = flat
    first[...] = flat[: first.shape[0]]
    second[...] = flat[first.shape[0] :]


def fetch_kernel(*refs):
    sources, gain, outs, (scale, gain_v, sems) = refs[:3], refs[3], refs[4:7], refs[7:]
    copies = fetch([(gain, gain_v), *zip(sources, outs)], sems)
    copies[0].wait()
    scale[...] = gain_v[...].astype(F32).reshape(1, -1)
    for copy in copies[1:]:
        copy.wait()


def own_kernel(mine, near, own_w, near_w, joined, hidden):
    tokens = joined.shape[0]
    tile = min(256, tokens)
    for at in range(0, tokens, tile):
        rows = pl.ds(at, tile)
        hidden[rows, :] = (
            joined[rows, :].astype(F32)
            + dot(mine[rows, :], own_w[...])
            + dot(near[rows, :], near_w[...])
        )


def ffn_kernel(groups, at, *refs):
    flats, wouts = refs[: groups - 2], refs[groups - 2 : 2 * (groups - 2)]
    hidden_v, scale, up_v, down_v, own, even, odd, scratch = refs[2 * (groups - 2) :]
    mine = lax.axis_index("ffn")
    rows, cols = own.shape
    hidden = hidden_v[pl.ds(at, rows), :]
    for flat, wout in zip(flats, wouts):
        hidden = hidden + dot(flat[...], wout[...])
    scratch[...] = hidden
    second = row_norm(hidden, scale[...]).astype(BF16)
    expanded = jax.nn.gelu(dot(second, up_v[...])).astype(BF16)
    for j in sorted(range(groups), key=lambda j: -(j % 2)):
        target = pl.ds(pl.multiple_of((mine ^ j) * cols, cols), cols)
        piece = dot(expanded, down_v[:, target])
        if j == 0:
            own[...] = piece + scratch[:, target]
        elif j % 2:
            odd[:, pl.ds((j // 2) * cols, cols)] = piece.astype(BF16)
        else:
            even[:, pl.ds((j // 2 - 1) * cols, cols)] = piece


def final_kernel(*refs):
    out = refs[-1]
    at = 0
    for i in range(2):
        own, near, far = refs[3 * i : 3 * i + 3]
        rows, cols = own.shape
        place = pl.ds(at, rows)
        at += rows
        out[place, :] = (
            own[...] + near[:, :cols].astype(F32) + far[...].astype(F32)
        ).astype(BF16)


def flip(array, axis, bit):
    size = lax.axis_size(axis)
    return lax.ppermute(array, axis, [(i, i ^ bit) for i in range(size)])


def gather_flips(array, axis):
    size = lax.axis_size(axis)
    parts = {0: array}
    bit = size // 2
    while bit:
        for k in list(parts):
            parts[k ^ bit] = flip(parts[k], axis, bit)
        bit //= 2
    return [parts[k] for k in range(size)]


def grant(mebibytes):
    return pltpu.CompilerParams(vmem_limit_bytes=mebibytes << 20)


def shaped(shape, dtype):
    return jax.ShapeDtypeStruct(shape, dtype)


def in_hbm(array):
    return pltpu.with_memory_space_constraint(array, pltpu.HBM)


def exchange(array):
    return lax.all_to_all(array, "seq", split_axis=0, concat_axis=0, tiled=True)


def on_device(
    child_feat,
    parent_feat,
    child_parent,
    owner,
    log_gate,
    norm_gain,
    w_query,
    w_key,
    w_value,
    head_gain,
    w_out,
    ffn_gain,
    w_up,
    w_down,
):
    blocks = lax.axis_size("seq")
    groups = lax.axis_size("ffn")
    heads, slots = log_gate.shape
    cap = slots // blocks
    tokens, width = child_feat.shape
    share = w_query.shape[1]
    hd = share // heads
    cols = width // groups

    child_feat, parent_feat, w_query, w_key, w_value, w_up, w_down = map(
        in_hbm, (child_feat, parent_feat, w_query, w_key, w_value, w_up, w_down)
    )
    arrived = exchange(log_gate.reshape(heads, blocks, cap).transpose(1, 0, 2))
    if cap % LANES:
        arrived = arrived.transpose(1, 0, 2).reshape(heads, slots)
    wout_parts = gather_flips(w_out, "ffn")

    tiles = pl.cdiv(tokens, min(256, tokens))
    joined, q, k, v, taken, own = pl.pallas_call(
        functools.partial(pre_kernel, cap, blocks),
        out_shape=(
            shaped((tokens, width), BF16),
            shaped((tokens, share), BF16),
            shaped((tokens, share), BF16),
            shaped((tokens, share), BF16),
            shaped((tokens, slots), BF16),
            shaped((1, tokens), jnp.int32),
        ),
        in_specs=[HBM] * 8,
        out_specs=[VMEM] * 6,
        scratch_shapes=[
            pltpu.VMEM((tokens, width), BF16),
            pltpu.VMEM(parent_feat.shape, BF16),
            pltpu.VMEM((1, tokens), jnp.int32),
            pltpu.VMEM((1, tokens), jnp.int32),
            pltpu.VMEM((width,), BF16),
            pltpu.VMEM((3, width, share), BF16),
            pltpu.SemaphoreType.DMA((7 + tiles,)),
        ],
        name="pre",
        compiler_params=grant(20),
    )(
        child_feat,
        parent_feat,
        in_hbm(child_parent.reshape(1, tokens)),
        in_hbm(owner.reshape(1, tokens)),
        in_hbm(norm_gain),
        w_query,
        w_key,
        w_value,
    )

    half = blocks // 2
    seats = 8 * pl.cdiv(half, 8)
    sent = shaped((half * hd + 2 * seats, share), BF16)
    held = shaped((half, hd, share), F32)
    rate = shaped((seats, share), F32)
    c_lanes, c_rows, *made = pl.pallas_call(
        functools.partial(state_kernel, cap, blocks, hd),
        out_shape=(shaped((tokens, share), F32), shaped((8, tokens), F32)) + (sent, held, rate) * 2,
        in_specs=[VMEM] * 5,
        out_specs=[VMEM] * 8,
        name="state",
        compiler_params=grant(12 if blocks <= 8 else 24),
    )(taken, arrived, k, v, own)
    scans = [made[:3], made[3:]]

    inside = pl.pallas_call(
        functools.partial(inside_kernel, hd),
        out_shape=shaped((tokens, share), F32),
        in_specs=[VMEM] * 6,
        out_specs=VMEM,
        name="inside",
        compiler_params=grant(12),
    )(q, k, v, c_lanes, c_rows, own)

    bits = [1 << i for i in range(blocks.bit_length() - 1)]
    for bit in bits:
        for g in range(2):
            came = flip(scans[g][0], "seq", bit)
            if bit == bits[-1]:
                scans[g] = [came, *scans[g][1:]]
                continue
            scans[g] = pl.pallas_call(
                functools.partial(step_kernel, bit, hd, bit == 1),
                out_shape=(sent, held, rate, held, rate),
                in_specs=[VMEM] * len(scans[g]),
                out_specs=[VMEM] * 5,
                compiler_params=grant(6 if blocks <= 8 else 24),
            )(came, *scans[g][1:])

    split = tokens * SPLIT // 16
    sizes = (split, tokens - split)
    scratch = [
        pltpu.VMEM((tokens, half * share), BF16),
        pltpu.VMEM((half * share, share), BF16),
    ]
    earlier, carried = pl.pallas_call(
        functools.partial(outside_kernel, bits[-1], range(half), hd),
        out_shape=(shaped((tokens, share), F32), shaped((hd, share), F32)),
        in_specs=[VMEM] * 7,
        out_specs=[VMEM] * 2,
        scratch_shapes=scratch,
        name="outside0",
        compiler_params=grant(8 if blocks <= 8 else 40),
    )(*scans[0], q, own)
    flat, *flats = pl.pallas_call(
        functools.partial(outside_kernel, bits[-1], range(half, blocks), hd),
        out_shape=tuple(shaped((rows, share), BF16) for rows in (tokens,) + sizes),
        in_specs=[VMEM] * 12,
        out_specs=[VMEM] * 3,
        scratch_shapes=scratch,
        name="outside1",
        compiler_params=grant(8 if blocks <= 8 else 40),
    )(*scans[1], q, own, carried, earlier, c_lanes, inside, head_gain.reshape(1, share))

    fetched = pl.pallas_call(
        fetch_kernel,
        out_shape=(
            pltpu.VMEM(w_out.shape, BF16),
            pltpu.VMEM(w_up.shape, BF16),
            pltpu.VMEM(w_down.shape, BF16),
            pltpu.VMEM((1, width), F32),
        ),
        in_specs=[HBM] * 4,
        out_specs=[VMEM] * 4,
        scratch_shapes=[pltpu.VMEM((width,), BF16), pltpu.SemaphoreType.DMA((4,))],
        name="fetch",
        compiler_params=grant(2),
    )(in_hbm(w_out), w_up, w_down, in_hbm(ffn_gain))

    near_flat = flip(flat, "ffn", 1)
    parts = [gather_flips(part, "ffn") for part in flats]
    hidden = pl.pallas_call(
        own_kernel,
        out_shape=pltpu.VMEM((tokens, width), F32),
        in_specs=[VMEM] * 5,
        out_specs=VMEM,
        name="own",
        compiler_params=grant(6),
    )(flat, near_flat, fetched[0], wout_parts[1], joined)
    finals = []
    for i, rows in enumerate(sizes):
        kept, even, odd = pl.pallas_call(
            functools.partial(ffn_kernel, groups, i * split),
            out_shape=(
                shaped((rows, cols), F32),
                shaped((rows, max(groups // 2 - 1, 1) * cols), F32),
                shaped((rows, groups // 2 * cols), BF16),
            ),
            in_specs=[VMEM] * (2 * groups),
            out_specs=[VMEM] * 3,
            scratch_shapes=[pltpu.VMEM((rows, width), F32)],
            compiler_params=grant(10),
        )(*parts[i][2:], *wout_parts[2:], hidden, fetched[3], *fetched[1:3])
        near = flip(odd, "ffn", 1)
        pieces = {
            j: (
                even[:, (j // 2 - 1) * cols : j // 2 * cols]
                + near[:, j // 2 * cols : (j // 2 + 1) * cols].astype(F32)
            )
            for j in range(2, groups, 2)
        }
        far = [flip(pieces[j].astype(BF16), "ffn", j) for j in pieces]
        far = far[0] if len(far) == 1 else sum(part.astype(F32) for part in far)
        finals += [kept, near, far]
    return pl.pallas_call(
        final_kernel,
        out_shape=shaped((tokens, cols), BF16),
        in_specs=[VMEM] * 6,
        out_specs=VMEM,
        name="final",
        compiler_params=grant(8),
    )(*finals)


def solution(mesh):
    in_specs = (
        P("seq", None),
        P("seq", None),
        P("seq"),
        P("seq", None),
        P("ffn", "seq"),
        P(),
        P(None, "ffn"),
        P(None, "ffn"),
        P(None, "ffn"),
        P("ffn"),
        P("ffn", None),
        P(),
        P(None, "ffn"),
        P("ffn", None),
    )

    return jax.shard_map(
        on_device, mesh=mesh, in_specs=in_specs, out_specs=P("seq", "ffn"), check_vma=False
    )
```
